256 devices in a mesh: gx: 16 (over x_hi, z), gy: 16 (over y, x_lo, core).
Axes of the slice: x: 4 (x_hi: 2, x_lo: 2; x = x_hi * 2 + x_lo), y: 4, z: 8, core: 2. Of those that a mesh axis runs over, the one named last changes fastest.
Arguments:
- tangent: float32 [256, 256, 512], P('gx', 'gy'), may hold values from -6 to 6
- hessian: bfloat16 [5, 5, 256, 256, 512], P(None, None, 'gx', 'gy'), may hold values from -1.5 to 8, as said below
- kernel_rows: float32 [5, 17], replicated, may hold values from -1 to 1
- kernel_cols: float32 [5, 17], replicated, may hold values from -1 to 1
- kernel_depth: bfloat16 [5, 17], replicated, may hold values from -1 to 1
Outputs:
- hessian_product: float32 [256, 256, 512], P('gx', 'gy')
The draws below stay inside these ranges and needn't reach their ends.
Inputs may be any that keep to these rules, and one draw needn't show every extreme that they name: `hessian`: Off-diagonal entries lie within -1.5 to 1.5; diagonal entries are positive, between 0.3 and 8.
All inputs are finite; a program needn't handle non-finite values.
Results may differ from the reference program's by a relative error of at most 0.0022.
Values sent between devices are 32-bit elements; how exact they have to be, the bound alone decides.
No kernel may reach another device: no remote copies, remote signals or barrier semaphores. Data moves between devices by JAX's collectives and lax.ppermute only.
A program may use at most 128 MiB of HBM per device.

```python
import jax
import jax.numpy as jnp
from jax import lax

NZ = 512
RADIUS = 8
DENSITIES = 5
TAPS = 17
NX = 256
NY = 256


def draw_hessian(key, part):
    first_key, second_key = jax.random.split(jax.random.fold_in(key, 17))
    full_shape = (DENSITIES, DENSITIES, NX, NY, NZ)
    diag_shape = (DENSITIES, 1, NX, NY, NZ)
    offdiag = jnp.clip(0.3 * jax.random.normal(first_key, full_shape, jnp.float32), -1.5, 1.5)
    diagonal = jnp.exp(jax.random.uniform(second_key, diag_shape, jnp.float32, jnp.log(0.5), jnp.log(5.0)))
    identity = jnp.eye(DENSITIES, dtype=jnp.float32)[:, :, None, None, None]
    return (offdiag * (1.0 - identity) + diagonal * identity).astype(jnp.bfloat16)


def levels(own_key, dims, cuts, least, high):
    def one(dim, parts):
        steps = jax.random.uniform(jax.random.fold_in(jax.random.fold_in(own_key, 6), dim), (parts,), jnp.float32, least / len(cuts), high / len(cuts))
        return jnp.repeat(jnp.exp(steps), dims[dim] // parts).reshape((-1,) + (1,) * (len(dims) - dim - 1))

    level = one(*cuts[0])
    for cut in cuts[1:]:
        level = level * one(*cut)
    return level


def noise(stream_key, shape, width, limit, shards=(), kind=jnp.bfloat16):
    drawn = width * jax.random.normal(stream_key, shape, jnp.float32)
    if shards:
        drawn = drawn * levels(stream_key, shape, shards, -0.22, 0.18)
    return jnp.clip(drawn, -limit, limit).astype(kind)


def setup_inputs(seed: int = 0) -> dict:
    seeds = jax.random.split(jax.random.key(seed), 6)
    return {
        "tangent": noise(seeds[0], (NX, NY, NZ), 1.0, 6.0, ((0, 16), (1, 16)), jnp.float32),
        "hessian": draw_hessian(jax.random.fold_in(seeds[5], 71), 0),
        "kernel_rows": noise(seeds[2], (DENSITIES, TAPS), 0.24, 1.0, (), jnp.float32),
        "kernel_cols": noise(seeds[3], (DENSITIES, TAPS), 0.24, 1.0, (), jnp.float32),
        "kernel_depth": noise(seeds[4], (DENSITIES, TAPS), 0.24, 1.0),
    }


def lateral_forward(field, weights, axis_number):
    total = jnp.zeros_like(field)
    for shift_tap in range(2 * RADIUS + 1):
        total = total + weights[shift_tap] * jnp.roll(field, RADIUS - shift_tap, axis_number)
    return total


def lateral_transpose(field, weights, axis_number):
    total = jnp.zeros_like(field)
    for shift_tap in range(2 * RADIUS + 1):
        total = total + weights[shift_tap] * jnp.roll(field, shift_tap - RADIUS, axis_number)
    return total


def widen(field):
    rounded = lax.optimization_barrier(field.astype(jnp.bfloat16))
    return rounded.astype(jnp.float32)


def depth_forward(field, weights):
    padded = jnp.pad(field, ((0, 0), (0, 0), (RADIUS, RADIUS)))
    total = jnp.zeros(field.shape, jnp.float32)
    for shift_tap in range(2 * RADIUS + 1):
        total = total + weights[shift_tap].astype(jnp.float32) * padded[:, :, shift_tap:shift_tap + NZ]
    return total


def depth_transpose(field, weights):
    padded = jnp.pad(field, ((0, 0), (0, 0), (RADIUS, RADIUS)))
    total = jnp.zeros(field.shape, jnp.float32)
    for shift_tap in range(2 * RADIUS + 1):
        start = 2 * RADIUS - shift_tap
        total = total + weights[shift_tap].astype(jnp.float32) * padded[:, :, start:start + NZ]
    return total


def reference(tangent, hessian, kernel_rows, kernel_cols, kernel_depth):
    densities = []
    for density in range(DENSITIES):
        field = lateral_forward(tangent, kernel_rows[density], 0)
        field = lateral_forward(field, kernel_cols[density], 1)
        densities.append(depth_forward(widen(field), kernel_depth[density]))
    result = jnp.zeros_like(tangent)
    for density in range(DENSITIES):
        gradient = jnp.zeros_like(tangent)
        for other in range(DENSITIES):
            gradient = gradient + hessian[density, other].astype(jnp.float32) * densities[other]
        field = depth_transpose(widen(gradient), kernel_depth[density])
        field = lateral_transpose(field, kernel_rows[density], 0)
        field = lateral_transpose(field, kernel_cols[density], 1)
        result = result + field
    return result
```

```python
import functools

import jax
import jax.numpy as jnp
import numpy as np
from jax import lax
from jax.experimental import pallas as pl
from jax.experimental.pallas import tpu as pltpu
from jax.sharding import PartitionSpec as P

RADIUS = 8
DENSITIES = 5
TAPS = 2 * RADIUS + 1
TILE = 16
CELLS = TILE * TILE


def piece_cells():
    inner = list(range(TILE))
    outer = list(range(-RADIUS, 0)) + list(range(TILE, TILE + RADIUS))
    west, east = list(range(-RADIUS, 0)), list(range(TILE, TILE + RADIUS))
    blocks = [
        (inner, inner),
        (outer, inner),
        (inner, west),
        (inner, east),
        (outer, west),
        (outer, east),
    ]
    return blocks


def cell_arrays():
    rows, cols = [], []
    for block_rows, block_cols in piece_cells():
        for row in block_rows:
            for col in block_cols:
                rows.append(row)
                cols.append(col)
    return np.array(rows, np.int32), np.array(cols, np.int32)


def taps_at(weights, offsets):
    shape = (DENSITIES,) + (1,) * offsets.ndim
    total = jnp.zeros((DENSITIES,) + offsets.shape, jnp.float32)
    for tap in range(TAPS):
        total = jnp.where((offsets == tap - RADIUS)[None], weights[:, tap].reshape(shape), total)
    return total


def split(values):
    high = lax.reduce_precision(values, 8, 7)
    return high.astype(jnp.bfloat16), (values - high).astype(jnp.bfloat16)


def lateral_matrices(kernel_rows, kernel_cols):
    rows, cols = cell_arrays()
    tile = np.arange(TILE, dtype=np.int32)
    by_row = taps_at(kernel_rows, jnp.asarray(rows[None, :] - tile[:, None]))
    by_col = taps_at(kernel_cols, jnp.asarray(cols[None, :] - tile[:, None]))
    product = by_row[:, :, None, :] * by_col[:, None, :, :]
    return split(product.reshape(DENSITIES * CELLS, rows.size))


def lateral_transposes(kernel_rows, kernel_cols):
    span = np.arange(-RADIUS, TILE + RADIUS, dtype=np.int32)
    tile = np.repeat(np.arange(TILE, dtype=np.int32), TILE)
    tile_cols = np.tile(np.arange(TILE, dtype=np.int32), TILE)
    by_row = taps_at(kernel_rows, jnp.asarray(span[:, None] - tile[None, :]))
    by_col = taps_at(kernel_cols, jnp.asarray(span[:, None] - tile_cols[None, :]))
    by_row = jnp.moveaxis(by_row, 0, 1).reshape(span.size, DENSITIES * CELLS)
    by_col = jnp.moveaxis(by_col, 0, 1).reshape(span.size, DENSITIES * CELLS)
    parts = []
    for block_rows, block_cols in piece_cells():
        low, high = block_cols[0] + RADIUS, block_cols[-1] + RADIUS + 1
        if block_rows[0] == 0:
            chosen = by_row[RADIUS : RADIUS + TILE]
        else:
            chosen = jnp.concatenate([by_row[:RADIUS], by_row[RADIUS + TILE :]], 0)
        product = chosen[:, None, :] * by_col[None, low:high, :]
        parts.append(product.reshape(-1, DENSITIES * CELLS))
    return split(jnp.concatenate(parts, 0))


def depth_bands(kernel_depth, depth):
    weights = kernel_depth.astype(jnp.float32)
    block = 128
    span = np.arange(3 * block)[None, :] - block - np.arange(block)[:, None]
    count = depth // block
    out = []
    for sign in (-1, 1):
        window = taps_at(weights, jnp.asarray((sign * span).astype(np.int32))).astype(jnp.bfloat16)
        rows = []
        for index in range(count):
            low, high = (index - 1) * block, (index + 2) * block
            part = window[:, :, max(0, -low) : 3 * block - max(0, high - depth)]
            rows.append(
                jnp.pad(part, ((0, 0), (0, 0), (max(0, low), max(0, depth - high))))
            )
        out.append(jnp.concatenate(rows, 1))
    return out


def halves(values):
    high = values.astype(jnp.bfloat16)
    return high, (values - high.astype(jnp.float32)).astype(jnp.bfloat16)


def dot3(left_high, left_low, right_high, right_low):
    left = jnp.concatenate([left_high, left_low, left_high], 1)
    right = jnp.concatenate([right_high, right_high, right_low], 0)
    return jnp.dot(left, right, preferred_element_type=jnp.float32)


def near_kernel(own, north, south, west, east, wh, wl, out, xh, xl):
    @pl.when(pl.program_id(0) == 0)
    def _():
        depth = own.shape[-1]
        start = 0
        for ref in (own, north, south, west, east):
            size = ref.shape[0] * ref.shape[1]
            high, low = halves(ref[...].reshape(size, depth))
            xh[start : start + size] = high
            xl[start : start + size] = low
            start += size

    out[...] = dot3(wh[...], wl[...], xh[...], xl[...])


def near(pieces, wh, wl):
    depth = pieces[0].shape[-1]
    keys = 3 * CELLS
    whole = lambda a: pl.BlockSpec(a.shape, lambda i: (0,) * a.ndim)
    weights = pl.BlockSpec((CELLS, keys), lambda i: (i, 0))
    return pl.pallas_call(
        near_kernel,
        grid=(DENSITIES,),
        out_shape=jax.ShapeDtypeStruct((DENSITIES * CELLS, depth), jnp.float32),
        in_specs=[whole(a) for a in pieces] + [weights, weights],
        out_specs=pl.BlockSpec((CELLS, depth), lambda i: (i, 0)),
        scratch_shapes=[pltpu.VMEM((keys, depth), jnp.bfloat16)] * 2,
        compiler_params=pltpu.CompilerParams(vmem_limit_bytes=32 << 20),
        cost_estimate=pl.CostEstimate(
            flops=6 * DENSITIES * CELLS * keys * depth, bytes_accessed=10 << 20, transcendentals=0
        ),
        name="near",
    )(*pieces, wh, wl)


def middle_kernel(
    partial, corner_w, corner_e, wh, wl, hessian, bands, bands_t, th, tl, out_w, out_e, bh, bl, xh, xl, dens, low
):
    depth = partial.shape[-1]
    half = CELLS // 2
    for start, ref in ((0, corner_w), (half, corner_e)):
        high, rest = halves(ref[...].reshape(half, depth))
        xh[start : start + half] = high
        xl[start : start + half] = rest
    for b in range(DENSITIES):
        rows = slice(b * CELLS, (b + 1) * CELLS)
        lateral = partial[rows] + dot3(wh[rows], wl[rows], xh[...], xl[...])
        dens[b] = jnp.dot(lateral.astype(jnp.bfloat16), bands[b], preferred_element_type=jnp.float32)
    total = None
    for a in range(DENSITIES):
        for r in range(TILE):
            cells = slice(r * TILE, (r + 1) * TILE)
            grad = hessian[a, 0, r].astype(jnp.float32) * dens[0, cells]
            for b in range(1, DENSITIES):
                grad = grad + hessian[a, b, r].astype(jnp.float32) * dens[b, cells]
            low[a, cells] = grad.astype(jnp.bfloat16)
        back = jnp.dot(low[a], bands_t[a], preferred_element_type=jnp.float32)
        rows = slice(a * CELLS, (a + 1) * CELLS)
        high, rest = halves(back)
        bh[rows] = high
        bl[rows] = rest
        term = dot3(th[:, rows], tl[:, rows], high, rest)
        total = term if total is None else total + term
    out_w[...] = total[:half].reshape(out_w.shape)
    out_e[...] = total[half:].reshape(out_e.shape)


def middle(partial, corner_w, corner_e, wh, wl, hessian, bands, bands_t, th, tl):
    depth = partial.shape[-1]
    edge = jax.ShapeDtypeStruct(corner_w.shape, jnp.float32)
    back = jax.ShapeDtypeStruct((DENSITIES * CELLS, depth), jnp.bfloat16)
    vmem = pl.BlockSpec(memory_space=pltpu.VMEM)
    return pl.pallas_call(
        middle_kernel,
        out_shape=[edge, edge, back, back],
        in_specs=[vmem] * 10,
        out_specs=[vmem] * 4,
        scratch_shapes=[
            pltpu.VMEM((CELLS, depth), jnp.bfloat16),
            pltpu.VMEM((CELLS, depth), jnp.bfloat16),
            pltpu.VMEM((DENSITIES, CELLS, depth), jnp.float32),
            pltpu.VMEM((DENSITIES, CELLS, depth), jnp.bfloat16),
        ],
        compiler_params=pltpu.CompilerParams(vmem_limit_bytes=48 << 20),
        cost_estimate=pl.CostEstimate(
            flops=DENSITIES * CELLS * depth * (12 * CELLS + 4 * depth), bytes_accessed=16 << 20, transcendentals=0
        ),
        name="middle",
    )(partial, corner_w, corner_e, wh, wl, hessian, bands, bands_t, th, tl)


def spread_kernel(th, tl, bh, bl, *outs):
    total = dot3(th[...], tl[...], bh[...], bl[...])
    start = 0
    for out in outs:
        size = out.shape[0] * out.shape[1]
        out[...] = total[start : start + size].reshape(out.shape)
        start += size


def spread(th, tl, bh, bl, shapes):
    depth = bh.shape[-1]
    vmem = pl.BlockSpec(memory_space=pltpu.VMEM)
    return pl.pallas_call(
        spread_kernel,
        out_shape=[jax.ShapeDtypeStruct(s + (depth,), jnp.float32) for s in shapes],
        in_specs=[vmem] * 4,
        out_specs=[vmem] * len(shapes),
        compiler_params=pltpu.CompilerParams(vmem_limit_bytes=32 << 20),
        cost_estimate=pl.CostEstimate(
            flops=6 * th.shape[0] * th.shape[1] * depth, bytes_accessed=6 << 20, transcendentals=0
        ),
        name="spread",
    )(th, tl, bh, bl)


def shift(cells, axis, step):
    count = lax.axis_size(axis)
    return lax.ppermute(cells, axis, [(i, (i + step) % count) for i in range(count)])


def per_device(tangent, hessian, kernel_rows, kernel_cols, kernel_depth):
    span_rows, span_cols, depth = tangent.shape
    reach = RADIUS

    north = shift(tangent[reach:], "gx", 1)
    south = shift(tangent[:reach], "gx", -1)
    west = shift(tangent[:, reach:], "gy", 1)
    east = shift(tangent[:, :reach], "gy", -1)

    wh, wl = lateral_matrices(kernel_rows, kernel_cols)
    th, tl = lateral_transposes(kernel_rows, kernel_cols)
    bands, bands_t = depth_bands(kernel_depth, depth)

    sides = jnp.concatenate([north, south], 0)
    corner_w = shift(sides[:, reach:], "gy", 1)
    corner_e = shift(sides[:, :reach], "gy", -1)

    inner, outer = slice(0, 3 * CELLS), slice(3 * CELLS, 4 * CELLS)
    partial = near((tangent, north, south, west, east), wh[:, inner], wl[:, inner])
    to_w, to_e, bh, bl = middle(
        partial, corner_w, corner_e, wh[:, outer], wl[:, outer], hessian, bands, bands_t, th[outer], tl[outer]
    )
    from_e = shift(to_w, "gy", -1)
    from_w = shift(to_e, "gy", 1)

    sides = slice(2 * CELLS, 3 * CELLS)
    edge_w, edge_e = spread(th[sides], tl[sides], bh, bl, [(span_rows, reach)] * 2)
    edge_from_e = shift(edge_w, "gy", -1)
    edge_from_w = shift(edge_e, "gy", 1)

    rest = slice(0, 2 * CELLS)
    own, around = spread(th[rest], tl[rest], bh, bl, [(span_rows, span_cols)] * 2)
    around = around + jnp.concatenate([from_w, from_e], 1)
    side_from_s = shift(around[:reach], "gx", -1)
    side_from_n = shift(around[reach:], "gx", 1)
    own = own + jnp.concatenate([edge_from_w, edge_from_e], 1)
    return own + jnp.concatenate([side_from_n, side_from_s], 0)


def solution(mesh):
    return jax.shard_map(
        per_device,
        mesh=mesh,
        in_specs=(P("gx", "gy", None), P(None, None, "gx", "gy", None), P(), P(), P()),
        out_specs=P("gx", "gy", None),
        check_vma=False,
    )
```

```python
import jax
import jax.numpy as jnp
import numpy as np
from jax import lax
from jax.experimental import pallas as pl
from jax.experimental.pallas import tpu as pltpu
from jax.sharding import PartitionSpec as P

RADIUS = 8
DENSITIES = 5
TAPS = 2 * RADIUS + 1
TILE = 16
CELLS = TILE * TILE


def piece_cells():
    inner = list(range(TILE))
    outer = list(range(-RADIUS, 0)) + list(range(TILE, TILE + RADIUS))
    west, east = list(range(-RADIUS, 0)), list(range(TILE, TILE + RADIUS))
    blocks = [
        (inner, inner),
        (outer, inner),
        (inner, west),
        (inner, east),
        (outer, west),
        (outer, east),
    ]
    return blocks


def cell_arrays():
    rows, cols = [], []
    for block_rows, block_cols in piece_cells():
        for row in block_rows:
            for col in block_cols:
                rows.append(row)
                cols.append(col)
    return np.array(rows, np.int32), np.array(cols, np.int32)


def offset_tables():
    rows, cols = cell_arrays()
    tile = np.arange(TILE, dtype=np.int32)
    span = np.arange(-RADIUS, TILE + RADIUS, dtype=np.int32)
    tile_rows, tile_cols = np.repeat(tile, TILE), np.tile(tile, TILE)
    return (
        rows[None, :] - tile[:, None],
        cols[None, :] - tile[:, None],
        span[:, None] - tile_rows[None, :],
        span[:, None] - tile_cols[None, :],
    )


def taps_at(weights, density, offsets):
    total = jnp.zeros(offsets.shape, jnp.float32)
    for tap in range(TAPS):
        total = jnp.where(offsets == tap - RADIUS, weights[density, tap], total)
    return total


def taps_of_all(weights, offsets):
    totals = [jnp.zeros(offsets.shape, jnp.float32)] * DENSITIES
    for tap in range(TAPS):
        here = offsets == tap - RADIUS
        totals = [jnp.where(here, weights[a, tap], totals[a]) for a in range(DENSITIES)]
    return totals


LANES = 128


def build_kernel(
    kr, kc, kd, row_off, col_off, row_span, col_span, nh, nl, ch, cl, sh, sl, rh, rl, eh, el, bands, bands_t
):
    def put(high_ref, low_ref, start, lanes, values):
        high, low = halves(values)
        high_ref[start : start + TILE, lanes] = high
        low_ref[start : start + TILE, lanes] = low

    def forward(high_ref, low_ref, first):
        def chunk(index, carry):
            source = pl.ds(pl.multiple_of(first + index * LANES, LANES), LANES)
            lanes = pl.ds(pl.multiple_of(index * LANES, LANES), LANES)
            by_row = taps_of_all(kr, row_off[:, source])
            by_col = taps_of_all(kc, col_off[:, source])
            for a in range(DENSITIES):
                for r in range(TILE):
                    put(high_ref, low_ref, a * CELLS + r * TILE, lanes, by_row[a][r : r + 1] * by_col[a])
            return carry

        lax.fori_loop(0, high_ref.shape[1] // LANES, chunk, 0)

    forward(nh, nl, 0)
    forward(ch, cl, 3 * CELLS)

    def transposes(index, carry):
        density = index // 2
        source = pl.ds(pl.multiple_of((index % 2) * LANES, LANES), LANES)
        lanes = pl.ds(pl.multiple_of(index * LANES, LANES), LANES)
        by_row = taps_at(kr, density, row_span[:, source])
        by_col = taps_at(kc, density, col_span[:, source])
        row = lambda r: by_row[r + RADIUS : r + RADIUS + 1]
        inner = list(range(TILE))
        outer = list(range(-RADIUS, 0)) + list(range(TILE, TILE + RADIUS))
        mid = by_col[RADIUS : RADIUS + TILE]
        for place, r in enumerate(inner + outer):
            put(rh, rl, place * TILE, lanes, row(r) * mid)
        for high_ref, low_ref, rows in ((sh, sl, inner), (eh, el, outer)):
            for side, edge in enumerate((by_col[:RADIUS], by_col[RADIUS + TILE :])):
                for pair in range(TILE // 2):
                    both = [row(rows[2 * pair]) * edge, row(rows[2 * pair + 1]) * edge]
                    put(high_ref, low_ref, side * CELLS // 2 + pair * TILE, lanes, jnp.concatenate(both, 0))
        return carry

    lax.fori_loop(0, DENSITIES * CELLS // LANES, transposes, 0)

    depth = bands.shape[-1]
    count = depth // LANES

    def band(density, carry):
        for ref, sign in ((bands, 1), (bands_t, -1)):
            ref[density] = jnp.zeros((depth, depth), jnp.bfloat16)
            for start in range(0, LANES, TILE):
                shape = (TILE, LANES)
                offsets = sign * (
                    start + lax.broadcasted_iota(jnp.int32, shape, 0) - lax.broadcasted_iota(jnp.int32, shape, 1)
                )
                part = taps_at(kd, density, offsets).astype(jnp.bfloat16)
                for block in range(count):
                    base = block * LANES
                    ref[density, base + start : base + start + TILE, base : base + LANES] = part
                for step, near_edge in ((1, start == 0), (-1, start == LANES - TILE)):
                    if near_edge:
                        part = taps_at(kd, density, offsets + sign * step * LANES).astype(jnp.bfloat16)
                        for block in range(count):
                            if 0 <= block + step < count:
                                base, across = (block + step) * LANES, block * LANES
                                ref[density, base + start : base + start + TILE, across : across + LANES] = part
        return carry

    lax.fori_loop(0, DENSITIES, band, 0)


def build(kernel_rows, kernel_cols, kernel_depth, depth):
    cells = DENSITIES * CELLS
    shapes = [(cells, 3 * CELLS)] * 2 + [(cells, CELLS)] * 2
    shapes += [(CELLS, cells)] * 2 + [(2 * CELLS, cells)] * 2 + [(CELLS, cells)] * 2
    shapes += [(DENSITIES, depth, depth)] * 2
    vmem = pl.BlockSpec(memory_space=pltpu.VMEM)
    smem = pl.BlockSpec(memory_space=pltpu.SMEM)
    return pl.pallas_call(
        build_kernel,
        out_shape=[jax.ShapeDtypeStruct(s, jnp.bfloat16) for s in shapes],
        in_specs=[smem] * 3 + [vmem] * 4,
        out_specs=[vmem] * len(shapes),
        compiler_params=pltpu.CompilerParams(vmem_limit_bytes=24 << 20),
        cost_estimate=pl.CostEstimate(flops=30 << 20, bytes_accessed=16 << 20, transcendentals=0),
        name="build",
    )(
        kernel_rows,
        kernel_cols,
        kernel_depth.astype(jnp.float32),
        *[jnp.asarray(table.astype(np.int32)) for table in offset_tables()],
    )


def halves(values):
    high = values.astype(jnp.bfloat16)
    return high, (values - high.astype(jnp.float32)).astype(jnp.bfloat16)


def dot3(left_high, left_low, right_high, right_low):
    left = jnp.concatenate([left_high, left_low, left_high], 1)
    right = jnp.concatenate([right_high, right_high, right_low], 0)
    return jnp.dot(left, right, preferred_element_type=jnp.float32)


def near_kernel(own, north, south, west, east, wh, wl, out, xh, xl):
    depth = own.shape[-1]
    start = 0
    for ref in (own, north, south, west, east):
        size = ref.shape[0] * ref.shape[1]
        high, low = halves(ref[...].reshape(size, depth))
        xh[start : start + size] = high
        xl[start : start + size] = low
        start += size

    def density(index, carry):
        rows = pl.ds(pl.multiple_of(index * CELLS, CELLS), CELLS)
        out[rows] = dot3(wh[rows], wl[rows], xh[...], xl[...])
        return carry

    lax.fori_loop(0, DENSITIES, density, 0)


def near(pieces, wh, wl):
    depth = pieces[0].shape[-1]
    keys = 3 * CELLS
    vmem = pl.BlockSpec(memory_space=pltpu.VMEM)
    return pl.pallas_call(
        near_kernel,
        out_shape=jax.ShapeDtypeStruct((DENSITIES * CELLS, depth), jnp.float32),
        in_specs=[vmem] * 7,
        out_specs=vmem,
        scratch_shapes=[pltpu.VMEM((keys, depth), jnp.bfloat16)] * 2,
        compiler_params=pltpu.CompilerParams(vmem_limit_bytes=16 << 20),
        cost_estimate=pl.CostEstimate(
            flops=6 * DENSITIES * CELLS * keys * depth, bytes_accessed=10 << 20, transcendentals=0
        ),
        name="near",
    )(*pieces, wh, wl)


def middle_kernel(
    partial, corner_w, corner_e, wh, wl, bands, bands_t, th, tl, hessian_hbm, out_w, out_e, bh, bl,
    xh, xl, dens, low, hessian, sems
):
    depth = partial.shape[-1]
    half = CELLS // 2
    copies = [
        pltpu.make_async_copy(hessian_hbm.at[a], hessian.at[a], sems.at[a]) for a in range(DENSITIES)
    ]
    for copy in copies:
        copy.start()
    for start, ref in ((0, corner_w), (half, corner_e)):
        high, rest = halves(ref[...].reshape(half, depth))
        xh[start : start + half] = high
        xl[start : start + half] = rest
    for b in range(DENSITIES):
        rows = slice(b * CELLS, (b + 1) * CELLS)
        lateral = partial[rows] + dot3(wh[rows], wl[rows], xh[...], xl[...])
        dens[b] = jnp.dot(lateral.astype(jnp.bfloat16), bands[b], preferred_element_type=jnp.float32)
    for a in range(DENSITIES):
        copies[a].wait()
        for r in range(TILE):
            cells = slice(r * TILE, (r + 1) * TILE)
            grad = hessian[a, 0, r].astype(jnp.float32) * dens[0, cells]
            for b in range(1, DENSITIES):
                grad = grad + hessian[a, b, r].astype(jnp.float32) * dens[b, cells]
            low[a, cells] = grad.astype(jnp.bfloat16)
        back = jnp.dot(low[a], bands_t[a], preferred_element_type=jnp.float32)
        rows = slice(a * CELLS, (a + 1) * CELLS)
        high, rest = halves(back)
        bh[rows] = high
        bl[rows] = rest
    total = dot3(th[...], tl[...], bh[...], bl[...])
    out_w[...] = total[:half].reshape(out_w.shape)
    out_e[...] = total[half:].reshape(out_e.shape)


def middle(partial, corner_w, corner_e, wh, wl, bands, bands_t, th, tl, hessian):
    depth = partial.shape[-1]
    edge = jax.ShapeDtypeStruct(corner_w.shape, jnp.float32)
    back = jax.ShapeDtypeStruct((DENSITIES * CELLS, depth), jnp.bfloat16)
    vmem = pl.BlockSpec(memory_space=pltpu.VMEM)
    return pl.pallas_call(
        middle_kernel,
        out_shape=[edge, edge, back, back],
        in_specs=[vmem] * 9 + [pl.BlockSpec(memory_space=pl.ANY)],
        out_specs=[vmem] * 4,
        scratch_shapes=[
            pltpu.VMEM((CELLS, depth), jnp.bfloat16),
            pltpu.VMEM((CELLS, depth), jnp.bfloat16),
            pltpu.VMEM((DENSITIES, CELLS, depth), jnp.float32),
            pltpu.VMEM((DENSITIES, CELLS, depth), jnp.bfloat16),
            pltpu.VMEM(hessian.shape, jnp.bfloat16),
            pltpu.SemaphoreType.DMA((DENSITIES,)),
        ],
        compiler_params=pltpu.CompilerParams(vmem_limit_bytes=32 << 20),
        cost_estimate=pl.CostEstimate(
            flops=DENSITIES * CELLS * depth * (12 * CELLS + 4 * depth), bytes_accessed=16 << 20, transcendentals=0
        ),
        name="middle",
    )(partial, corner_w, corner_e, wh, wl, bands, bands_t, th, tl, hessian)


def spread_kernel(th, tl, bh, bl, *outs):
    total = dot3(th[...], tl[...], bh[...], bl[...])
    start = 0
    for out in outs:
        size = out.shape[0] * out.shape[1]
        out[...] = total[start : start + size].reshape(out.shape)
        start += size


def spread(th, tl, bh, bl, shapes):
    depth = bh.shape[-1]
    vmem = pl.BlockSpec(memory_space=pltpu.VMEM)
    return pl.pallas_call(
        spread_kernel,
        out_shape=[jax.ShapeDtypeStruct(s + (depth,), jnp.float32) for s in shapes],
        in_specs=[vmem] * 4,
        out_specs=[vmem] * len(shapes),
        compiler_params=pltpu.CompilerParams(vmem_limit_bytes=16 << 20),
        cost_estimate=pl.CostEstimate(
            flops=6 * th.shape[0] * th.shape[1] * depth, bytes_accessed=6 << 20, transcendentals=0
        ),
        name="spread",
    )(th, tl, bh, bl)


def shift(cells, axis, step):
    count = lax.axis_size(axis)
    return lax.ppermute(cells, axis, [(i, (i + step) % count) for i in range(count)])


def per_device(tangent, hessian, kernel_rows, kernel_cols, kernel_depth):
    span_rows, span_cols, depth = tangent.shape
    reach = RADIUS

    north = shift(tangent[reach:], "gx", 1)
    south = shift(tangent[:reach], "gx", -1)
    west = shift(tangent[:, reach:], "gy", 1)
    east = shift(tangent[:, :reach], "gy", -1)

    nh, nl, ch, cl, sh, sl, rh, rl, eh, el, bands, bands_t = build(kernel_rows, kernel_cols, kernel_depth, depth)

    sides = jnp.concatenate([north, south], 0)
    corner_w = shift(sides[:, reach:], "gy", 1)
    corner_e = shift(sides[:, :reach], "gy", -1)

    partial = near((tangent, north, south, west, east), nh, nl)
    to_w, to_e, bh, bl = middle(partial, corner_w, corner_e, ch, cl, bands, bands_t, eh, el, hessian)
    from_e = shift(to_w, "gy", -1)
    from_w = shift(to_e, "gy", 1)

    edge_w, edge_e = spread(sh, sl, bh, bl, [(span_rows, reach)] * 2)
    edge_from_e = shift(edge_w, "gy", -1)
    edge_from_w = shift(edge_e, "gy", 1)

    own, around = spread(rh, rl, bh, bl, [(span_rows, span_cols)] * 2)
    around = around + jnp.concatenate([from_w, from_e], 1)
    side_from_s = shift(around[:reach], "gx", -1)
    side_from_n = shift(around[reach:], "gx", 1)
    own = own + jnp.concatenate([edge_from_w, edge_from_e], 1)
    return own + jnp.concatenate([side_from_n, side_from_s], 0)


def solution(mesh):
    return jax.shard_map(
        per_device,
        mesh=mesh,
        in_specs=(P("gx", "gy", None), P(None, None, "gx", "gy", None), P(), P(), P()),
        out_specs=P("gx", "gy", None),
        check_vma=False,
    )
```

```python
import functools

import jax
import jax.numpy as jnp
import numpy as np
from jax import lax
from jax.experimental import pallas as pl
from jax.experimental.pallas import tpu as pltpu
from jax.sharding import PartitionSpec as P

RADIUS = 8
DENSITIES = 5
TAPS = 2 * RADIUS + 1
TILE = 16
CELLS = TILE * TILE


def piece_cells():
    inner = list(range(TILE))
    outer = list(range(-RADIUS, 0)) + list(range(TILE, TILE + RADIUS))
    west, east = list(range(-RADIUS, 0)), list(range(TILE, TILE + RADIUS))
    blocks = [
        (inner, inner),
        (outer, inner),
        (inner, west),
        (inner, east),
        (outer, west),
        (outer, east),
    ]
    return blocks


def cell_arrays():
    rows, cols = [], []
    for block_rows, block_cols in piece_cells():
        for row in block_rows:
            for col in block_cols:
                rows.append(row)
                cols.append(col)
    return np.array(rows, np.int32), np.array(cols, np.int32)


def offset_tables():
    rows, cols = cell_arrays()
    tile = np.arange(TILE, dtype=np.int32)
    span = np.arange(-RADIUS, TILE + RADIUS, dtype=np.int32)
    tile_rows, tile_cols = np.repeat(tile, TILE), np.tile(tile, TILE)
    return (
        rows[None, :] - tile[:, None],
        cols[None, :] - tile[:, None],
        span[:, None] - tile_rows[None, :],
        span[:, None] - tile_cols[None, :],
    )


TURN = TILE + RADIUS


def side_is_right():
    return 1 - lax.rem(lax.axis_index("gy"), 2)


def taps_at(weights, density, offsets):
    total = jnp.zeros(offsets.shape, jnp.float32)
    for tap in range(TAPS):
        total = jnp.where(offsets == tap - RADIUS, weights[density, tap], total)
    return total


def taps_of_all(weights, offsets):
    totals = [jnp.zeros(offsets.shape, jnp.float32)] * DENSITIES
    for tap in range(TAPS):
        here = offsets == tap - RADIUS
        totals = [jnp.where(here, weights[a, tap], totals[a]) for a in range(DENSITIES)]
    return totals


LANES = 128


def build_kernel(
    kr, kc, kd, row_off, col_off, row_span, col_span,
    nh, nl, ch, cl, th, tl, bands, bands_t
):
    turn = TURN * side_is_right()

    def put(high_ref, low_ref, start, lanes, values):
        high, low = halves(values)
        high_ref[start : start + TILE, lanes] = high
        low_ref[start : start + TILE, lanes] = low

    def forward(high_ref, low_ref, first, side):
        def chunk(index, carry):
            toward = turn * ((index == side).astype(jnp.int32) - (index == side + 1).astype(jnp.int32))
            source = pl.ds(pl.multiple_of(first + index * LANES, LANES), LANES)
            lanes = pl.ds(pl.multiple_of(index * LANES, LANES), LANES)
            by_row = taps_of_all(kr, row_off[:, source])
            by_col = taps_of_all(kc, col_off[:, source] + toward)
            for a in range(DENSITIES):
                for r in range(TILE):
                    put(high_ref, low_ref, a * CELLS + r * TILE, lanes, by_row[a][r : r + 1] * by_col[a])
            return carry

        lax.fori_loop(0, high_ref.shape[1] // LANES, chunk, 0)

    forward(nh, nl, 0, 4)
    forward(ch, cl, 3 * CELLS, 0)

    def transposes(index, carry):
        density = index // 2
        source = pl.ds(pl.multiple_of((index % 2) * LANES, LANES), LANES)
        lanes = pl.ds(pl.multiple_of(index * LANES, LANES), LANES)
        by_row = taps_at(kr, density, row_span[:, source])
        place = lax.broadcasted_iota(jnp.int32, (TILE + 2 * RADIUS, LANES), 0)
        toward = jnp.where(place < RADIUS, turn, jnp.where(place < TILE + RADIUS, 0, -turn))
        by_col = taps_at(kc, density, col_span[:, source] + toward)
        row = lambda r: by_row[r + RADIUS : r + RADIUS + 1]
        inner = list(range(TILE))
        outer = list(range(-RADIUS, 0)) + list(range(TILE, TILE + RADIUS))
        mid = by_col[RADIUS : RADIUS + TILE]
        for place, r in enumerate(inner + outer):
            put(th, tl, place * TILE, lanes, row(r) * mid)
        for base, rows in ((2 * CELLS, inner), (3 * CELLS, outer)):
            for side, edge in enumerate((by_col[:RADIUS], by_col[RADIUS + TILE :])):
                for pair in range(TILE // 2):
                    both = [row(rows[2 * pair]) * edge, row(rows[2 * pair + 1]) * edge]
                    put(th, tl, base + side * CELLS // 2 + pair * TILE, lanes, jnp.concatenate(both, 0))
        return carry

    lax.fori_loop(0, DENSITIES * CELLS // LANES, transposes, 0)

    depth = bands.shape[-1]
    count = depth // LANES

    def band(density, carry):
        for ref, sign in ((bands, 1), (bands_t, -1)):
            ref[density] = jnp.zeros((depth, depth), jnp.bfloat16)
            for start in range(0, LANES, TILE):
                shape = (TILE, LANES)
                offsets = sign * (
                    start + lax.broadcasted_iota(jnp.int32, shape, 0) - lax.broadcasted_iota(jnp.int32, shape, 1)
                )
                part = taps_at(kd, density, offsets).astype(jnp.bfloat16)
                for block in range(count):
                    base = block * LANES
                    ref[density, base + start : base + start + TILE, base : base + LANES] = part
                for step, near_edge in ((1, start == 0), (-1, start == LANES - TILE)):
                    if near_edge:
                        part = taps_at(kd, density, offsets + sign * step * LANES).astype(jnp.bfloat16)
                        for block in range(count):
                            if 0 <= block + step < count:
                                base, across = (block + step) * LANES, block * LANES
                                ref[density, base + start : base + start + TILE, across : across + LANES] = part
        return carry

    lax.fori_loop(0, DENSITIES, band, 0)


def build(kernel_rows, kernel_cols, kernel_depth, depth):
    cells = DENSITIES * CELLS
    shapes = [(cells, 3 * CELLS)] * 2 + [(cells, CELLS)] * 2
    shapes += [(4 * CELLS, cells)] * 2
    shapes += [(DENSITIES, depth, depth)] * 2
    vmem = pl.BlockSpec(memory_space=pltpu.VMEM)
    smem = pl.BlockSpec(memory_space=pltpu.SMEM)
    return pl.pallas_call(
        build_kernel,
        out_shape=[jax.ShapeDtypeStruct(s, jnp.bfloat16) for s in shapes],
        in_specs=[smem] * 3 + [vmem] * 4,
        out_specs=[vmem] * len(shapes),
        compiler_params=pltpu.CompilerParams(vmem_limit_bytes=24 << 20),
        cost_estimate=pl.CostEstimate(flops=30 << 20, bytes_accessed=16 << 20, transcendentals=0),
        name="build",
    )(
        kernel_rows,
        kernel_cols,
        kernel_depth.astype(jnp.float32),
        *[jnp.asarray(table.astype(np.int32)) for table in offset_tables()],
    )


def halves(values):
    high = values.astype(jnp.bfloat16)
    return high, (values - high.astype(jnp.float32)).astype(jnp.bfloat16)


def dot3(left_high, left_low, right_high, right_low):
    left = jnp.concatenate([left_high, left_low, left_high], 1)
    right = jnp.concatenate([right_high, right_high, right_low], 0)
    return jnp.dot(left, right, preferred_element_type=jnp.float32)


def near_kernel(own, north, south, side_a, side_b, wh, wl, out, xh, xl):
    depth = own.shape[-1]
    start = 0
    for ref in (own, north, south, side_a, side_b):
        size = ref.shape[0] * ref.shape[1]
        high, low = halves(ref[...].reshape(size, depth))
        xh[start : start + size] = high
        xl[start : start + size] = low
        start += size

    def density(index, carry):
        rows = pl.ds(pl.multiple_of(index * CELLS, CELLS), CELLS)
        out[rows] = dot3(wh[rows], wl[rows], xh[...], xl[...])
        return carry

    lax.fori_loop(0, DENSITIES, density, 0)


def near(pieces, wh, wl):
    depth = pieces[0].shape[-1]
    keys = 3 * CELLS
    vmem = pl.BlockSpec(memory_space=pltpu.VMEM)
    return pl.pallas_call(
        near_kernel,
        out_shape=jax.ShapeDtypeStruct((DENSITIES * CELLS, depth), jnp.float32),
        in_specs=[vmem] * 7,
        out_specs=vmem,
        scratch_shapes=[pltpu.VMEM((keys, depth), jnp.bfloat16)] * 2,
        compiler_params=pltpu.CompilerParams(vmem_limit_bytes=16 << 20),
        cost_estimate=pl.CostEstimate(
            flops=6 * DENSITIES * CELLS * keys * depth, bytes_accessed=10 << 20, transcendentals=0
        ),
        name="near",
    )(*pieces, wh, wl)


def middle_kernel(
    partial, corner_a, corner_b, wh, wl, bands, bands_t, th, tl, hessian, out_a, out_b, bh, bl,
    xh, xl, dens, low
):
    depth = partial.shape[-1]
    half = CELLS // 2
    for start, ref in ((0, corner_a), (half, corner_b)):
        high, rest = halves(ref[...].reshape(half, depth))
        xh[start : start + half] = high
        xl[start : start + half] = rest
    for b in range(DENSITIES):
        rows = slice(b * CELLS, (b + 1) * CELLS)
        lateral = partial[rows] + dot3(wh[rows], wl[rows], xh[...], xl[...])
        dens[b] = jnp.dot(lateral.astype(jnp.bfloat16), bands[b], preferred_element_type=jnp.float32)
    for a in range(DENSITIES):
        for r in range(TILE):
            cells = slice(r * TILE, (r + 1) * TILE)
            grad = hessian[a, 0, r].astype(jnp.float32) * dens[0, cells]
            for b in range(1, DENSITIES):
                grad = grad + hessian[a, b, r].astype(jnp.float32) * dens[b, cells]
            low[a, cells] = grad.astype(jnp.bfloat16)
        back = jnp.dot(low[a], bands_t[a], preferred_element_type=jnp.float32)
        rows = slice(a * CELLS, (a + 1) * CELLS)
        high, rest = halves(back)
        bh[rows] = high
        bl[rows] = rest
    corners = slice(3 * CELLS, 4 * CELLS)
    total = dot3(th[corners], tl[corners], bh[...], bl[...])
    out_a[...] = total[:half].reshape(out_a.shape)
    out_b[...] = total[half:].reshape(out_b.shape)


def middle(partial, corner_a, corner_b, wh, wl, bands, bands_t, th, tl, hessian):
    depth = partial.shape[-1]
    edge = jax.ShapeDtypeStruct(corner_a.shape, jnp.float32)
    back = jax.ShapeDtypeStruct((DENSITIES * CELLS, depth), jnp.bfloat16)
    vmem = pl.BlockSpec(memory_space=pltpu.VMEM)
    return pl.pallas_call(
        middle_kernel,
        out_shape=[edge, edge, back, back],
        in_specs=[vmem] * 10,
        out_specs=[vmem] * 4,
        scratch_shapes=[
            pltpu.VMEM((CELLS, depth), jnp.bfloat16),
            pltpu.VMEM((CELLS, depth), jnp.bfloat16),
            pltpu.VMEM((DENSITIES, CELLS, depth), jnp.float32),
            pltpu.VMEM((DENSITIES, CELLS, depth), jnp.bfloat16),
        ],
        compiler_params=pltpu.CompilerParams(vmem_limit_bytes=24 << 20),
        cost_estimate=pl.CostEstimate(
            flops=DENSITIES * CELLS * depth * (12 * CELLS + 4 * depth), bytes_accessed=16 << 20, transcendentals=0
        ),
        name="middle",
    )(partial, corner_a, corner_b, wh, wl, bands, bands_t, th, tl, hessian)


def spread_kernel(group, th, tl, bh, bl, *outs):
    rows = slice(group * CELLS, (group + 1) * CELLS)
    total = dot3(th[rows], tl[rows], bh[...], bl[...])
    start = 0
    for out in outs:
        size = out.shape[0] * out.shape[1]
        out[...] = total[start : start + size].reshape(out.shape)
        start += size


def spread(group, th, tl, bh, bl, shapes):
    depth = bh.shape[-1]
    vmem = pl.BlockSpec(memory_space=pltpu.VMEM)
    return pl.pallas_call(
        functools.partial(spread_kernel, group),
        out_shape=[jax.ShapeDtypeStruct(s + (depth,), jnp.float32) for s in shapes],
        in_specs=[vmem] * 4,
        out_specs=[vmem] * len(shapes),
        compiler_params=pltpu.CompilerParams(vmem_limit_bytes=16 << 20),
        cost_estimate=pl.CostEstimate(
            flops=6 * CELLS * th.shape[1] * depth, bytes_accessed=6 << 20, transcendentals=0
        ),
        name="spread",
    )(th, tl, bh, bl)


def shift(cells, axis, step):
    count = lax.axis_size(axis)
    return lax.ppermute(cells, axis, [(i, (i + step) % count) for i in range(count)])


def swap_a(cells):
    count = lax.axis_size("gy")
    return lax.ppermute(cells, "gy", [(j, j ^ 1) for j in range(count)])


def swap_b(cells):
    count = lax.axis_size("gy")
    return lax.ppermute(cells, "gy", [(j, (j + (1 if j % 2 else -1)) % count) for j in range(count)])


def per_device(tangent, hessian, kernel_rows, kernel_cols, kernel_depth):
    span_rows, span_cols, depth = tangent.shape
    reach = RADIUS
    right = side_is_right()

    def side_cols(cells, place):
        return lax.dynamic_slice_in_dim(cells, place * reach, reach, 1)

    def joined(from_a, from_b):
        left, other = jnp.concatenate([from_a, from_b], 1), jnp.concatenate([from_b, from_a], 1)
        return jnp.where(right == 1, other, left)

    north = shift(tangent[reach:], "gx", 1)
    south = shift(tangent[:reach], "gx", -1)
    side_b = swap_b(side_cols(tangent, 1 - right))
    side_a = swap_a(side_cols(tangent, right))

    nh, nl, ch, cl, th, tl, bands, bands_t = build(kernel_rows, kernel_cols, kernel_depth, depth)

    sides = jnp.concatenate([north, south], 0)
    corner_b = swap_b(side_cols(sides, 1 - right))
    corner_a = swap_a(side_cols(sides, right))

    partial = near((tangent, north, south, side_a, side_b), nh, nl)
    to_a, to_b, bh, bl = middle(partial, corner_a, corner_b, ch, cl, bands, bands_t, th, tl, hessian)
    from_b = swap_b(to_b)
    from_a = swap_a(to_a)

    edge_a, edge_b = spread(2, th, tl, bh, bl, [(span_rows, reach)] * 2)
    edge_from_b = swap_b(edge_b)
    edge_from_a = swap_a(edge_a)

    (around,) = spread(1, th, tl, bh, bl, [(span_rows, span_cols)])
    around = around + joined(from_a, from_b)
    side_from_s = shift(around[:reach], "gx", -1)
    side_from_n = shift(around[reach:], "gx", 1)

    around, bh, bl = lax.optimization_barrier((around, bh, bl))
    (own,) = spread(0, th, tl, bh, bl, [(span_rows, span_cols)])
    own = lax.optimization_barrier(own + joined(edge_from_a, edge_from_b))
    return own + jnp.concatenate([side_from_n, side_from_s], 0)


def solution(mesh):
    return jax.shard_map(
        per_device,
        mesh=mesh,
        in_specs=(P("gx", "gy", None), P(None, None, "gx", "gy", None), P(), P(), P()),
        out_specs=P("gx", "gy", None),
        check_vma=False,
    )
```

```python
import functools

import jax
import jax.numpy as jnp
from jax import lax
from jax.experimental import pallas as pl
from jax.experimental.pallas import tpu as pltpu
from jax.sharding import PartitionSpec as P

RADIUS = 8
DENSITIES = 5
TAPS = 2 * RADIUS + 1
TILE = 16
CELLS = TILE * TILE


LANES = 128
TURN = TILE + RADIUS


def side_is_right():
    return 1 - lax.rem(lax.axis_index("gy"), 2)


def taps_at(weights, first, density, offsets):
    total = jnp.zeros(offsets.shape, jnp.float32)
    for tap in range(TAPS):
        total = jnp.where(offsets == tap - RADIUS, weights[first + density, tap], total)
    return total


def taps_of_all(weights, first, offsets):
    totals = [jnp.zeros(offsets.shape, jnp.float32)] * DENSITIES
    for tap in range(TAPS):
        here = offsets == tap - RADIUS
        totals = [jnp.where(here, weights[first + a, tap], totals[a]) for a in range(DENSITIES)]
    return totals


ROWS, COLS, DEPTH = 0, DENSITIES, 2 * DENSITIES


def build_kernel(weights, nh, nl, ch, cl, th, tl, bands, bands_t):
    right = side_is_right()
    iota = lambda shape, dim: lax.broadcasted_iota(jnp.int32, shape, dim)

    def put(high_ref, low_ref, start, lanes, values):
        high, low = halves(values)
        high_ref[start : start + TILE, lanes] = high
        low_ref[start : start + TILE, lanes] = low

    def forward(high_ref, low_ref, first):
        def chunk(index, carry):
            lanes = pl.ds(pl.multiple_of(index * LANES, LANES), LANES)
            group, half = (first + index) // 2, (first + index) % 2
            lane, tile_place = iota((TILE, LANES), 1), iota((TILE, LANES), 0)
            wide, slim = lane >> 4, lane >> 3
            row = jnp.where(group == 2, slim, jnp.where(slim < RADIUS, slim - RADIUS, slim + RADIUS))
            row = jnp.where(group == 1, wide - RADIUS + TURN * half, row)
            row = jnp.where(group == 0, wide + RADIUS * half, row)
            side = half + right - 2 * half * right
            col = jnp.where(group < 2, lane & 15, (lane & 7) - RADIUS + TURN * side)
            by_row = taps_of_all(weights, ROWS, row - tile_place)
            by_col = taps_of_all(weights, COLS, col - tile_place)
            for a in range(DENSITIES):
                for r in range(TILE):
                    put(high_ref, low_ref, a * CELLS + r * TILE, lanes, by_row[a][r : r + 1] * by_col[a])
            return carry

        lax.fori_loop(0, high_ref.shape[1] // LANES, chunk, 0)

    forward(nh, nl, 0)
    forward(ch, cl, 6)

    def transposes(index, carry):
        density, half = index // 2, index % 2
        lanes = pl.ds(pl.multiple_of(index * LANES, LANES), LANES)
        shape = (TILE + 2 * RADIUS, LANES)
        place, lane = iota(shape, 0), iota(shape, 1)
        turn = TURN * right
        turned = place - RADIUS + jnp.where(place < RADIUS, turn, jnp.where(place < TILE + RADIUS, 0, -turn))
        by_row = taps_at(weights, ROWS, density, place - RADIUS - (lane >> 4) - RADIUS * half)
        by_col = taps_at(weights, COLS, density, turned - (lane & 15))
        row = lambda r: by_row[r + RADIUS : r + RADIUS + 1]
        inner = list(range(TILE))
        outer = list(range(-RADIUS, 0)) + list(range(TILE, TILE + RADIUS))
        mid = by_col[RADIUS : RADIUS + TILE]
        for place, r in enumerate(inner + outer):
            put(th, tl, place * TILE, lanes, row(r) * mid)
        for base, rows in ((2 * CELLS, inner), (3 * CELLS, outer)):
            for side, edge in enumerate((by_col[:RADIUS], by_col[RADIUS + TILE :])):
                for pair in range(TILE // 2):
                    both = [row(rows[2 * pair]) * edge, row(rows[2 * pair + 1]) * edge]
                    put(th, tl, base + side * CELLS // 2 + pair * TILE, lanes, jnp.concatenate(both, 0))
        return carry

    lax.fori_loop(0, DENSITIES * CELLS // LANES, transposes, 0)

    depth = bands.shape[-1]
    count = depth // LANES

    def band(density, carry):
        for ref, sign in ((bands, 1), (bands_t, -1)):
            ref[density] = jnp.zeros((depth, depth), jnp.bfloat16)
            for start in range(0, LANES, TILE):
                shape = (TILE, LANES)
                offsets = sign * (
                    start + iota(shape, 0) - iota(shape, 1)
                )
                part = taps_at(weights, DEPTH, density, offsets).astype(jnp.bfloat16)
                for block in range(count):
                    base = block * LANES
                    ref[density, base + start : base + start + TILE, base : base + LANES] = part
                for step, near_edge in ((1, start == 0), (-1, start == LANES - TILE)):
                    if near_edge:
                        part = taps_at(weights, DEPTH, density, offsets + sign * step * LANES).astype(jnp.bfloat16)
                        for block in range(count):
                            if 0 <= block + step < count:
                                base, across = (block + step) * LANES, block * LANES
                                ref[density, base + start : base + start + TILE, across : across + LANES] = part
        return carry

    lax.fori_loop(0, DENSITIES, band, 0)


def build(kernel_rows, kernel_cols, kernel_depth, depth):
    cells = DENSITIES * CELLS
    shapes = [(cells, 3 * CELLS)] * 2 + [(cells, CELLS)] * 2
    shapes += [(4 * CELLS, cells)] * 2
    shapes += [(DENSITIES, depth, depth)] * 2
    vmem = pl.BlockSpec(memory_space=pltpu.VMEM)
    smem = pl.BlockSpec(memory_space=pltpu.SMEM)
    return pl.pallas_call(
        build_kernel,
        out_shape=[jax.ShapeDtypeStruct(s, jnp.bfloat16) for s in shapes],
        in_specs=[smem],
        out_specs=[vmem] * len(shapes),
        compiler_params=pltpu.CompilerParams(vmem_limit_bytes=24 << 20),
        cost_estimate=pl.CostEstimate(flops=30 << 20, bytes_accessed=16 << 20, transcendentals=0),
        name="build",
    )(jnp.concatenate([kernel_rows, kernel_cols, kernel_depth.astype(jnp.float32)], 0))


def halves(values):
    high = values.astype(jnp.bfloat16)
    return high, (values - high.astype(jnp.float32)).astype(jnp.bfloat16)


def dot3(left_high, left_low, right_high, right_low):
    left = jnp.concatenate([left_high, left_low, left_high], 1)
    right = jnp.concatenate([right_high, right_high, right_low], 0)
    return jnp.dot(left, right, preferred_element_type=jnp.float32)


def near_kernel(own, north, south, side_a, side_b, wh, wl, out, xh, xl):
    depth = own.shape[-1]
    start = 0
    for ref in (own, north, south, side_a, side_b):
        size = ref.shape[0] * ref.shape[1]
        high, low = halves(ref[...].reshape(size, depth))
        xh[start : start + size] = high
        xl[start : start + size] = low
        start += size

    def density(index, carry):
        rows = pl.ds(pl.multiple_of(index * CELLS, CELLS), CELLS)
        out[rows] = dot3(wh[rows], wl[rows], xh[...], xl[...])
        return carry

    lax.fori_loop(0, DENSITIES, density, 0)


def near(pieces, wh, wl):
    depth = pieces[0].shape[-1]
    keys = 3 * CELLS
    vmem = pl.BlockSpec(memory_space=pltpu.VMEM)
    return pl.pallas_call(
        near_kernel,
        out_shape=jax.ShapeDtypeStruct((DENSITIES * CELLS, depth), jnp.float32),
        in_specs=[vmem] * 7,
        out_specs=vmem,
        scratch_shapes=[pltpu.VMEM((keys, depth), jnp.bfloat16)] * 2,
        compiler_params=pltpu.CompilerParams(vmem_limit_bytes=16 << 20),
        cost_estimate=pl.CostEstimate(
            flops=6 * DENSITIES * CELLS * keys * depth, bytes_accessed=10 << 20, transcendentals=0
        ),
        name="near",
    )(*pieces, wh, wl)


def middle_kernel(
    partial, corner_a, corner_b, wh, wl, bands, bands_t, th, tl, hessian, out_a, out_b, bh, bl,
    xh, xl, dens, low
):
    depth = partial.shape[-1]
    half = CELLS // 2
    for start, ref in ((0, corner_a), (half, corner_b)):
        high, rest = halves(ref[...].reshape(half, depth))
        xh[start : start + half] = high
        xl[start : start + half] = rest
    for b in range(DENSITIES):
        rows = slice(b * CELLS, (b + 1) * CELLS)
        lateral = partial[rows] + dot3(wh[rows], wl[rows], xh[...], xl[...])
        dens[b] = jnp.dot(lateral.astype(jnp.bfloat16), bands[b], preferred_element_type=jnp.float32)
    for a in range(DENSITIES):
        for r in range(TILE):
            cells = slice(r * TILE, (r + 1) * TILE)
            grad = hessian[a, 0, r].astype(jnp.float32) * dens[0, cells]
            for b in range(1, DENSITIES):
                grad = grad + hessian[a, b, r].astype(jnp.float32) * dens[b, cells]
            low[a, cells] = grad.astype(jnp.bfloat16)
        back = jnp.dot(low[a], bands_t[a], preferred_element_type=jnp.float32)
        rows = slice(a * CELLS, (a + 1) * CELLS)
        high, rest = halves(back)
        bh[rows] = high
        bl[rows] = rest
    corners = slice(3 * CELLS, 4 * CELLS)
    total = dot3(th[corners], tl[corners], bh[...], bl[...])
    out_a[...] = total[:half].reshape(out_a.shape)
    out_b[...] = total[half:].reshape(out_b.shape)


def middle(partial, corner_a, corner_b, wh, wl, bands, bands_t, th, tl, hessian):
    depth = partial.shape[-1]
    edge = jax.ShapeDtypeStruct(corner_a.shape, jnp.float32)
    back = jax.ShapeDtypeStruct((DENSITIES * CELLS, depth), jnp.bfloat16)
    vmem = pl.BlockSpec(memory_space=pltpu.VMEM)
    return pl.pallas_call(
        middle_kernel,
        out_shape=[edge, edge, back, back],
        in_specs=[vmem] * 10,
        out_specs=[vmem] * 4,
        scratch_shapes=[
            pltpu.VMEM((CELLS, depth), jnp.bfloat16),
            pltpu.VMEM((CELLS, depth), jnp.bfloat16),
            pltpu.VMEM((DENSITIES, CELLS, depth), jnp.float32),
            pltpu.VMEM((DENSITIES, CELLS, depth), jnp.bfloat16),
        ],
        compiler_params=pltpu.CompilerParams(vmem_limit_bytes=24 << 20),
        cost_estimate=pl.CostEstimate(
            flops=DENSITIES * CELLS * depth * (12 * CELLS + 4 * depth), bytes_accessed=16 << 20, transcendentals=0
        ),
        name="middle",
    )(partial, corner_a, corner_b, wh, wl, bands, bands_t, th, tl, hessian)


def spread_kernel(group, th, tl, bh, bl, *outs):
    rows = slice(group * CELLS, (group + 1) * CELLS)
    total = dot3(th[rows], tl[rows], bh[...], bl[...])
    start = 0
    for out in outs:
        size = out.shape[0] * out.shape[1]
        out[...] = total[start : start + size].reshape(out.shape)
        start += size


def spread(group, th, tl, bh, bl, shapes):
    depth = bh.shape[-1]
    vmem = pl.BlockSpec(memory_space=pltpu.VMEM)
    return pl.pallas_call(
        functools.partial(spread_kernel, group),
        out_shape=[jax.ShapeDtypeStruct(s + (depth,), jnp.float32) for s in shapes],
        in_specs=[vmem] * 4,
        out_specs=[vmem] * len(shapes),
        compiler_params=pltpu.CompilerParams(vmem_limit_bytes=16 << 20),
        cost_estimate=pl.CostEstimate(
            flops=6 * CELLS * th.shape[1] * depth, bytes_accessed=6 << 20, transcendentals=0
        ),
        name="spread",
    )(th, tl, bh, bl)


def cut_kernel(tangent, last, first, side_a, side_b):
    right = side_is_right()
    cols = lambda place: pl.ds(pl.multiple_of(place * RADIUS, RADIUS), RADIUS)
    last[...] = tangent[RADIUS:]
    first[...] = tangent[:RADIUS]
    side_a[...] = tangent[:, cols(right)]
    side_b[...] = tangent[:, cols(1 - right)]


def cut(tangent):
    span_rows, span_cols, depth = tangent.shape
    shapes = [(RADIUS, span_cols)] * 2 + [(span_rows, RADIUS)] * 2
    vmem = pl.BlockSpec(memory_space=pltpu.VMEM)
    return pl.pallas_call(
        cut_kernel,
        out_shape=[jax.ShapeDtypeStruct(s + (depth,), jnp.float32) for s in shapes],
        in_specs=[vmem],
        out_specs=[vmem] * 4,
        compiler_params=pltpu.CompilerParams(vmem_limit_bytes=8 << 20),
        cost_estimate=pl.CostEstimate(flops=0, bytes_accessed=3 << 20, transcendentals=0),
        name="cut",
    )(tangent)


def shift(cells, axis, step):
    count = lax.axis_size(axis)
    return lax.ppermute(cells, axis, [(i, (i + step) % count) for i in range(count)])


def swap_a(cells):
    count = lax.axis_size("gy")
    return lax.ppermute(cells, "gy", [(j, j ^ 1) for j in range(count)])


def swap_b(cells):
    count = lax.axis_size("gy")
    return lax.ppermute(cells, "gy", [(j, (j + (1 if j % 2 else -1)) % count) for j in range(count)])


def per_device(tangent, hessian, kernel_rows, kernel_cols, kernel_depth):
    span_rows, span_cols, depth = tangent.shape
    reach = RADIUS
    right = side_is_right()

    def side_cols(cells, place):
        return jnp.where(place == 1, cells[:, reach:], cells[:, :reach])

    def joined(from_a, from_b):
        left, other = jnp.concatenate([from_a, from_b], 1), jnp.concatenate([from_b, from_a], 1)
        return jnp.where(right == 1, other, left)

    last, first, cols_a, cols_b = cut(tangent)
    north = shift(last, "gx", 1)
    south = shift(first, "gx", -1)
    side_b = swap_b(cols_b)
    side_a = swap_a(cols_a)

    nh, nl, ch, cl, th, tl, bands, bands_t = build(kernel_rows, kernel_cols, kernel_depth, depth)

    sides = jnp.concatenate([north, south], 0)
    corner_b = swap_b(side_cols(sides, 1 - right))
    corner_a = swap_a(side_cols(sides, right))

    partial = near((tangent, north, south, side_a, side_b), nh, nl)
    to_a, to_b, bh, bl = middle(partial, corner_a, corner_b, ch, cl, bands, bands_t, th, tl, hessian)
    from_b = swap_b(to_b)
    from_a = swap_a(to_a)

    edge_a, edge_b = spread(2, th, tl, bh, bl, [(span_rows, reach)] * 2)
    edge_from_b = swap_b(edge_b)
    edge_from_a = swap_a(edge_a)

    (around,) = spread(1, th, tl, bh, bl, [(span_rows, span_cols)])
    around = around + joined(from_a, from_b)
    side_from_s = shift(around[:reach], "gx", -1)
    side_from_n = shift(around[reach:], "gx", 1)

    around, bh, bl = lax.optimization_barrier((around, bh, bl))
    (own,) = spread(0, th, tl, bh, bl, [(span_rows, span_cols)])
    own = lax.optimization_barrier(own + joined(edge_from_a, edge_from_b))
    return own + jnp.concatenate([side_from_n, side_from_s], 0)


def solution(mesh):
    return jax.shard_map(
        per_device,
        mesh=mesh,
        in_specs=(P("gx", "gy", None), P(None, None, "gx", "gy", None), P(), P(), P()),
        out_specs=P("gx", "gy", None),
        check_vma=False,
    )
```

```python
import functools

import jax
import jax.numpy as jnp
from jax import lax
from jax.experimental import pallas as pl
from jax.experimental.pallas import tpu as pltpu
from jax.sharding import PartitionSpec as P

RADIUS = 8
DENSITIES = 5
TAPS = 2 * RADIUS + 1
TILE = 16
CELLS = TILE * TILE


LANES = 128
TURN = TILE + RADIUS


def side_is_right():
    return 1 - lax.rem(lax.axis_index("gy"), 2)


def taps_at(weights, density, offsets):
    total = jnp.zeros(offsets.shape, jnp.float32)
    for tap in range(TAPS):
        total = jnp.where(offsets == tap - RADIUS, weights[density, tap], total)
    return total


def taps_of_all(weights, offsets):
    totals = [jnp.zeros(offsets.shape, jnp.float32)] * DENSITIES
    for tap in range(TAPS):
        here = offsets == tap - RADIUS
        totals = [jnp.where(here, weights[a, tap], totals[a]) for a in range(DENSITIES)]
    return totals


def build_kernel(
    kr_hbm, kc_hbm, kd_hbm, nh, nl, ch, cl, th, tl, bands, bands_t, kr, kc, depth_taps, depth_row, sems
):
    copies = [
        pltpu.make_async_copy(kr_hbm, kr, sems.at[0]),
        pltpu.make_async_copy(kc_hbm, kc, sems.at[1]),
        pltpu.make_async_copy(kd_hbm, depth_taps, sems.at[2]),
    ]
    for copy in copies:
        copy.start()
    copies[2].wait()
    right = side_is_right()
    iota = lambda shape, dim: lax.broadcasted_iota(jnp.int32, shape, dim)

    depth_row[...] = jnp.zeros(depth_row.shape, jnp.float32)
    depth_row[:DENSITIES, :TAPS] = depth_taps[...].astype(jnp.float32)
    depth = bands.shape[-1]
    block = (LANES, LANES)
    ahead = iota(block, 1) - iota(block, 0)

    def band(density, carry):
        row = jnp.broadcast_to(depth_row[pl.ds(density, 1)], block)
        ring_t = pltpu.roll(row, LANES - RADIUS, 1, stride=1, stride_axis=0)
        for ref, ring in ((bands_t, ring_t), (bands, ring_t.T)):
            ref[density] = jnp.zeros((depth, depth), jnp.bfloat16)
            for step in (-1, 0, 1):
                here = jnp.abs(ahead + step * LANES) <= RADIUS
                part = jnp.where(here, ring, 0.0).astype(jnp.bfloat16)
                for start in range(0, depth, LANES):
                    across = start + step * LANES
                    if 0 <= across < depth:
                        ref[density, start : start + LANES, across : across + LANES] = part
        return carry

    lax.fori_loop(0, DENSITIES, band, 0)
    for copy in copies[:2]:
        copy.wait()

    def put(high_ref, low_ref, start, lanes, values):
        high, low = halves(values)
        high_ref[start : start + TILE, lanes] = high
        low_ref[start : start + TILE, lanes] = low

    def forward(high_ref, low_ref, first):
        def chunk(index, carry):
            lanes = pl.ds(pl.multiple_of(index * LANES, LANES), LANES)
            group, half = (first + index) // 2, (first + index) % 2
            lane, tile_place = iota((TILE, LANES), 1), iota((TILE, LANES), 0)
            wide, slim = lane >> 4, lane >> 3
            row = jnp.where(group == 2, slim, jnp.where(slim < RADIUS, slim - RADIUS, slim + RADIUS))
            row = jnp.where(group == 1, wide - RADIUS + TURN * half, row)
            row = jnp.where(group == 0, wide + RADIUS * half, row)
            side = half + right - 2 * half * right
            col = jnp.where(group < 2, lane & 15, (lane & 7) - RADIUS + TURN * side)
            by_row = taps_of_all(kr, row - tile_place)
            by_col = taps_of_all(kc, col - tile_place)
            for a in range(DENSITIES):
                for r in range(TILE):
                    put(high_ref, low_ref, a * CELLS + r * TILE, lanes, by_row[a][r : r + 1] * by_col[a])
            return carry

        lax.fori_loop(0, high_ref.shape[1] // LANES, chunk, 0)

    forward(nh, nl, 0)
    forward(ch, cl, 6)

    def transposes(index, carry):
        density, half = index // 2, index % 2
        lanes = pl.ds(pl.multiple_of(index * LANES, LANES), LANES)
        shape = (TILE + 2 * RADIUS, LANES)
        place, lane = iota(shape, 0), iota(shape, 1)
        turn = TURN * right
        turned = place - RADIUS + jnp.where(place < RADIUS, turn, jnp.where(place < TILE + RADIUS, 0, -turn))
        by_row = taps_at(kr, density, place - RADIUS - (lane >> 4) - RADIUS * half)
        by_col = taps_at(kc, density, turned - (lane & 15))
        row = lambda r: by_row[r + RADIUS : r + RADIUS + 1]
        inner = list(range(TILE))
        outer = list(range(-RADIUS, 0)) + list(range(TILE, TILE + RADIUS))
        mid = by_col[RADIUS : RADIUS + TILE]
        for place, r in enumerate(inner + outer):
            put(th, tl, place * TILE, lanes, row(r) * mid)
        for base, rows in ((2 * CELLS, inner), (3 * CELLS, outer)):
            for side, edge in enumerate((by_col[:RADIUS], by_col[RADIUS + TILE :])):
                for pair in range(TILE // 2):
                    both = [row(rows[2 * pair]) * edge, row(rows[2 * pair + 1]) * edge]
                    put(th, tl, base + side * CELLS // 2 + pair * TILE, lanes, jnp.concatenate(both, 0))
        return carry

    lax.fori_loop(0, DENSITIES * CELLS // LANES, transposes, 0)

def build(kernel_rows, kernel_cols, kernel_depth, depth):
    cells = DENSITIES * CELLS
    shapes = [(cells, 3 * CELLS)] * 2 + [(cells, CELLS)] * 2
    shapes += [(4 * CELLS, cells)] * 2
    shapes += [(DENSITIES, depth, depth)] * 2
    vmem = pl.BlockSpec(memory_space=pltpu.VMEM)
    hbm = pl.BlockSpec(memory_space=pltpu.HBM)
    return pl.pallas_call(
        build_kernel,
        out_shape=[jax.ShapeDtypeStruct(s, jnp.bfloat16) for s in shapes],
        in_specs=[hbm] * 3,
        out_specs=[vmem] * len(shapes),
        scratch_shapes=[
            pltpu.SMEM(kernel_rows.shape, jnp.float32),
            pltpu.SMEM(kernel_cols.shape, jnp.float32),
            pltpu.VMEM(kernel_depth.shape, jnp.bfloat16),
            pltpu.VMEM((RADIUS, LANES), jnp.float32),
            pltpu.SemaphoreType.DMA((3,)),
        ],
        compiler_params=pltpu.CompilerParams(vmem_limit_bytes=24 << 20),
        cost_estimate=pl.CostEstimate(flops=30 << 20, bytes_accessed=16 << 20, transcendentals=0),
        name="build",
    )(*[pltpu.with_memory_space_constraint(a, pltpu.HBM) for a in (kernel_rows, kernel_cols, kernel_depth)])


def halves(values):
    high = values.astype(jnp.bfloat16)
    return high, (values - high.astype(jnp.float32)).astype(jnp.bfloat16)


def dot3(left_high, left_low, right_high, right_low):
    left = jnp.concatenate([left_high, left_low, left_high], 1)
    right = jnp.concatenate([right_high, right_high, right_low], 0)
    return jnp.dot(left, right, preferred_element_type=jnp.float32)


def near_kernel(own, north, south, side_a, side_b, wh, wl, out, xh, xl):
    depth = own.shape[-1]
    start = 0
    for ref in (own, north, south, side_a, side_b):
        size = ref.shape[0] * ref.shape[1]
        high, low = halves(ref[...].reshape(size, depth))
        xh[start : start + size] = high
        xl[start : start + size] = low
        start += size

    def density(index, carry):
        rows = pl.ds(pl.multiple_of(index * CELLS, CELLS), CELLS)
        out[rows] = dot3(wh[rows], wl[rows], xh[...], xl[...])
        return carry

    lax.fori_loop(0, DENSITIES, density, 0)


def near(pieces, wh, wl):
    depth = pieces[0].shape[-1]
    keys = 3 * CELLS
    vmem = pl.BlockSpec(memory_space=pltpu.VMEM)
    return pl.pallas_call(
        near_kernel,
        out_shape=jax.ShapeDtypeStruct((DENSITIES * CELLS, depth), jnp.float32),
        in_specs=[vmem] * 7,
        out_specs=vmem,
        scratch_shapes=[pltpu.VMEM((keys, depth), jnp.bfloat16)] * 2,
        compiler_params=pltpu.CompilerParams(vmem_limit_bytes=16 << 20),
        cost_estimate=pl.CostEstimate(
            flops=6 * DENSITIES * CELLS * keys * depth, bytes_accessed=10 << 20, transcendentals=0
        ),
        name="near",
    )(*pieces, wh, wl)


def middle_kernel(
    partial, corner_a, corner_b, wh, wl, bands, bands_t, th, tl, hessian, out_a, out_b, bh, bl,
    xh, xl, dens, low
):
    depth = partial.shape[-1]
    half = CELLS // 2
    for start, ref in ((0, corner_a), (half, corner_b)):
        high, rest = halves(ref[...].reshape(half, depth))
        xh[start : start + half] = high
        xl[start : start + half] = rest
    for b in range(DENSITIES):
        rows = slice(b * CELLS, (b + 1) * CELLS)
        lateral = partial[rows] + dot3(wh[rows], wl[rows], xh[...], xl[...])
        dens[b] = jnp.dot(lateral.astype(jnp.bfloat16), bands[b], preferred_element_type=jnp.float32)
    for a in range(DENSITIES):
        for r in range(TILE):
            cells = slice(r * TILE, (r + 1) * TILE)
            grad = hessian[a, 0, r].astype(jnp.float32) * dens[0, cells]
            for b in range(1, DENSITIES):
                grad = grad + hessian[a, b, r].astype(jnp.float32) * dens[b, cells]
            low[a, cells] = grad.astype(jnp.bfloat16)
        back = jnp.dot(low[a], bands_t[a], preferred_element_type=jnp.float32)
        rows = slice(a * CELLS, (a + 1) * CELLS)
        high, rest = halves(back)
        bh[rows] = high
        bl[rows] = rest
    corners = slice(3 * CELLS, 4 * CELLS)
    total = dot3(th[corners], tl[corners], bh[...], bl[...])
    out_a[...] = total[:half].reshape(out_a.shape)
    out_b[...] = total[half:].reshape(out_b.shape)


def middle(partial, corner_a, corner_b, wh, wl, bands, bands_t, th, tl, hessian):
    depth = partial.shape[-1]
    edge = jax.ShapeDtypeStruct(corner_a.shape, jnp.float32)
    back = jax.ShapeDtypeStruct((DENSITIES * CELLS, depth), jnp.bfloat16)
    vmem = pl.BlockSpec(memory_space=pltpu.VMEM)
    return pl.pallas_call(
        middle_kernel,
        out_shape=[edge, edge, back, back],
        in_specs=[vmem] * 10,
        out_specs=[vmem] * 4,
        scratch_shapes=[
            pltpu.VMEM((CELLS, depth), jnp.bfloat16),
            pltpu.VMEM((CELLS, depth), jnp.bfloat16),
            pltpu.VMEM((DENSITIES, CELLS, depth), jnp.float32),
            pltpu.VMEM((DENSITIES, CELLS, depth), jnp.bfloat16),
        ],
        compiler_params=pltpu.CompilerParams(vmem_limit_bytes=24 << 20),
        cost_estimate=pl.CostEstimate(
            flops=DENSITIES * CELLS * depth * (12 * CELLS + 4 * depth), bytes_accessed=16 << 20, transcendentals=0
        ),
        name="middle",
    )(partial, corner_a, corner_b, wh, wl, bands, bands_t, th, tl, hessian)


def spread_kernel(group, th, tl, bh, bl, *outs):
    rows = slice(group * CELLS, (group + 1) * CELLS)
    total = dot3(th[rows], tl[rows], bh[...], bl[...])
    start = 0
    for out in outs:
        size = out.shape[0] * out.shape[1]
        out[...] = total[start : start + size].reshape(out.shape)
        start += size


def spread(group, th, tl, bh, bl, shapes):
    depth = bh.shape[-1]
    vmem = pl.BlockSpec(memory_space=pltpu.VMEM)
    return pl.pallas_call(
        functools.partial(spread_kernel, group),
        out_shape=[jax.ShapeDtypeStruct(s + (depth,), jnp.float32) for s in shapes],
        in_specs=[vmem] * 4,
        out_specs=[vmem] * len(shapes),
        compiler_params=pltpu.CompilerParams(vmem_limit_bytes=16 << 20),
        cost_estimate=pl.CostEstimate(
            flops=6 * CELLS * th.shape[1] * depth, bytes_accessed=6 << 20, transcendentals=0
        ),
        name="spread",
    )(th, tl, bh, bl)


def cut_kernel(tangent, *refs):
    outs, sems = refs[:-1], refs[-1]
    right = side_is_right()
    rows = lambda start: tangent.at[pl.ds(start, RADIUS)]
    cols = lambda place: tangent.at[:, pl.ds(pl.multiple_of(place * RADIUS, RADIUS), RADIUS)]
    sources = (rows(RADIUS), rows(0), cols(right), cols(1 - right), tangent)
    copies = [
        pltpu.make_async_copy(source, out, sems.at[index])
        for index, (source, out) in enumerate(zip(sources, outs))
    ]
    for copy in copies:
        copy.start()
    for copy in copies:
        copy.wait()


def cut(tangent):
    span_rows, span_cols, depth = tangent.shape
    shapes = [(RADIUS, span_cols)] * 2 + [(span_rows, RADIUS)] * 2 + [(span_rows, span_cols)]
    vmem = pl.BlockSpec(memory_space=pltpu.VMEM)
    return pl.pallas_call(
        cut_kernel,
        out_shape=[jax.ShapeDtypeStruct(s + (depth,), jnp.float32) for s in shapes],
        in_specs=[pl.BlockSpec(memory_space=pltpu.HBM)],
        out_specs=[vmem] * 5,
        scratch_shapes=[pltpu.SemaphoreType.DMA((5,))],
        compiler_params=pltpu.CompilerParams(vmem_limit_bytes=8 << 20),
        cost_estimate=pl.CostEstimate(flops=0, bytes_accessed=3 << 20, transcendentals=0),
        name="cut",
    )(pltpu.with_memory_space_constraint(tangent, pltpu.HBM))


def shift(cells, axis, step):
    count = lax.axis_size(axis)
    return lax.ppermute(cells, axis, [(i, (i + step) % count) for i in range(count)])


def swap_a(cells):
    count = lax.axis_size("gy")
    return lax.ppermute(cells, "gy", [(j, j ^ 1) for j in range(count)])


def swap_b(cells):
    count = lax.axis_size("gy")
    return lax.ppermute(cells, "gy", [(j, (j + (1 if j % 2 else -1)) % count) for j in range(count)])


def per_device(tangent, hessian, kernel_rows, kernel_cols, kernel_depth):
    span_rows, span_cols, depth = tangent.shape
    reach = RADIUS
    right = side_is_right()

    def side_cols(cells, place):
        return jnp.where(place == 1, cells[:, reach:], cells[:, :reach])

    def joined(from_a, from_b):
        left, other = jnp.concatenate([from_a, from_b], 1), jnp.concatenate([from_b, from_a], 1)
        return jnp.where(right == 1, other, left)

    last, first, cols_a, cols_b, tile = cut(tangent)
    north = shift(last, "gx", 1)
    south = shift(first, "gx", -1)
    side_b = swap_b(cols_b)
    side_a = swap_a(cols_a)

    nh, nl, ch, cl, th, tl, bands, bands_t = build(kernel_rows, kernel_cols, kernel_depth, depth)

    sides = jnp.concatenate([north, south], 0)
    corner_b = swap_b(side_cols(sides, 1 - right))
    corner_a = swap_a(side_cols(sides, right))

    partial = near((tile, north, south, side_a, side_b), nh, nl)
    to_a, to_b, bh, bl = middle(partial, corner_a, corner_b, ch, cl, bands, bands_t, th, tl, hessian)
    from_b = swap_b(to_b)
    from_a = swap_a(to_a)

    edge_a, edge_b = spread(2, th, tl, bh, bl, [(span_rows, reach)] * 2)
    edge_from_b = swap_b(edge_b)
    edge_from_a = swap_a(edge_a)

    (around,) = spread(1, th, tl, bh, bl, [(span_rows, span_cols)])
    around = around + joined(from_a, from_b)
    above, below = around[:reach], around[reach:]
    side_from_n = shift(below, "gx", 1)
    above, below = lax.optimization_barrier((above, below))
    side_from_s = shift(above, "gx", -1)

    around, bh, bl = lax.optimization_barrier((around, bh, bl))
    (own,) = spread(0, th, tl, bh, bl, [(span_rows, span_cols)])
    own = lax.optimization_barrier(own + joined(edge_from_a, edge_from_b))
    return own + jnp.concatenate([side_from_n, side_from_s], 0)


def solution(mesh):
    return jax.shard_map(
        per_device,
        mesh=mesh,
        in_specs=(P("gx", "gy", None), P(None, None, "gx", "gy", None), P(), P(), P()),
        out_specs=P("gx", "gy", None),
        check_vma=False,
    )
```

```python
import functools

import jax
import jax.numpy as jnp
from jax import lax
from jax.experimental import pallas as pl
from jax.experimental.pallas import tpu as pltpu
from jax.sharding import PartitionSpec as P

RADIUS = 8
DENSITIES = 5
TAPS = 2 * RADIUS + 1
TILE = 16
CELLS = TILE * TILE


LANES = 128
TURN = TILE + RADIUS


def side_is_right():
    return 1 - lax.rem(lax.axis_index("gy"), 2)


def taps_at(weights, density, offsets):
    total = jnp.zeros(offsets.shape, jnp.float32)
    for tap in range(TAPS):
        total = jnp.where(offsets == tap - RADIUS, weights[density, tap], total)
    return total


def taps_of_all(weights, offsets):
    totals = [jnp.zeros(offsets.shape, jnp.float32)] * DENSITIES
    for tap in range(TAPS):
        here = offsets == tap - RADIUS
        totals = [jnp.where(here, weights[a, tap], totals[a]) for a in range(DENSITIES)]
    return totals


def build_kernel(
    kr_hbm, kc_hbm, kd_hbm, nh, nl, ch, cl, th, tl, bands, bands_t, kr, kc, depth_taps, depth_row, sems
):
    copies = [
        pltpu.make_async_copy(kr_hbm, kr, sems.at[0]),
        pltpu.make_async_copy(kc_hbm, kc, sems.at[1]),
        pltpu.make_async_copy(kd_hbm, depth_taps, sems.at[2]),
    ]
    for copy in copies:
        copy.start()
    copies[2].wait()
    right = side_is_right()
    iota = lambda shape, dim: lax.broadcasted_iota(jnp.int32, shape, dim)

    depth_row[...] = jnp.zeros(depth_row.shape, jnp.float32)
    depth_row[:DENSITIES, :TAPS] = depth_taps[...].astype(jnp.float32)
    depth = bands.shape[-1]
    block = (LANES, LANES)
    ahead = iota(block, 1) - iota(block, 0)

    def band(density, carry):
        row = jnp.broadcast_to(depth_row[pl.ds(density, 1)], block)
        ring_t = pltpu.roll(row, LANES - RADIUS, 1, stride=1, stride_axis=0)
        for ref, ring in ((bands_t, ring_t), (bands, ring_t.T)):
            ref[density] = jnp.zeros((depth, depth), jnp.bfloat16)
            for step in (-1, 0, 1):
                here = jnp.abs(ahead + step * LANES) <= RADIUS
                part = jnp.where(here, ring, 0.0).astype(jnp.bfloat16)
                for start in range(0, depth, LANES):
                    across = start + step * LANES
                    if 0 <= across < depth:
                        ref[density, start : start + LANES, across : across + LANES] = part
        return carry

    lax.fori_loop(0, DENSITIES, band, 0)
    for copy in copies[:2]:
        copy.wait()

    def put(high_ref, low_ref, start, lanes, values):
        high, low = halves(values)
        high_ref[start : start + TILE, lanes] = high
        low_ref[start : start + TILE, lanes] = low

    def forward(high_ref, low_ref, first):
        def chunk(index, carry):
            lanes = pl.ds(pl.multiple_of(index * LANES, LANES), LANES)
            group, half = (first + index) // 2, (first + index) % 2
            lane, tile_place = iota((TILE, LANES), 1), iota((TILE, LANES), 0)
            wide, slim = lane >> 4, lane >> 3
            row = jnp.where(group == 2, slim, jnp.where(slim < RADIUS, slim - RADIUS, slim + RADIUS))
            row = jnp.where(group == 1, wide - RADIUS + TURN * half, row)
            row = jnp.where(group == 0, wide + RADIUS * half, row)
            side = half + right - 2 * half * right
            col = jnp.where(group < 2, lane & 15, (lane & 7) - RADIUS + TURN * side)
            by_row = taps_of_all(kr, row - tile_place)
            by_col = taps_of_all(kc, col - tile_place)
            for a in range(DENSITIES):
                for r in range(TILE):
                    put(high_ref, low_ref, a * CELLS + r * TILE, lanes, by_row[a][r : r + 1] * by_col[a])
            return carry

        lax.fori_loop(0, high_ref.shape[1] // LANES, chunk, 0)

    forward(nh, nl, 0)
    forward(ch, cl, 6)

    def transposes(index, carry):
        density, half = index // 2, index % 2
        lanes = pl.ds(pl.multiple_of(index * LANES, LANES), LANES)
        shape = (TILE + 2 * RADIUS, LANES)
        place, lane = iota(shape, 0), iota(shape, 1)
        turn = TURN * right
        turned = place - RADIUS + jnp.where(place < RADIUS, turn, jnp.where(place < TILE + RADIUS, 0, -turn))
        by_row = taps_at(kr, density, place - RADIUS - (lane >> 4) - RADIUS * half)
        by_col = taps_at(kc, density, turned - (lane & 15))
        row = lambda r: by_row[r + RADIUS : r + RADIUS + 1]
        inner = list(range(TILE))
        outer = list(range(-RADIUS, 0)) + list(range(TILE, TILE + RADIUS))
        mid = by_col[RADIUS : RADIUS + TILE]
        for place, r in enumerate(inner + outer):
            put(th, tl, place * TILE, lanes, row(r) * mid)
        for base, rows in ((2 * CELLS, inner), (3 * CELLS, outer)):
            for side, edge in enumerate((by_col[:RADIUS], by_col[RADIUS + TILE :])):
                for pair in range(TILE // 2):
                    both = [row(rows[2 * pair]) * edge, row(rows[2 * pair + 1]) * edge]
                    put(th, tl, base + side * CELLS // 2 + pair * TILE, lanes, jnp.concatenate(both, 0))
        return carry

    lax.fori_loop(0, DENSITIES * CELLS // LANES, transposes, 0)

def build(kernel_rows, kernel_cols, kernel_depth, depth):
    cells = DENSITIES * CELLS
    shapes = [(cells, 3 * CELLS)] * 2 + [(cells, CELLS)] * 2
    shapes += [(4 * CELLS, cells)] * 2
    shapes += [(DENSITIES, depth, depth)] * 2
    vmem = pl.BlockSpec(memory_space=pltpu.VMEM)
    hbm = pl.BlockSpec(memory_space=pltpu.HBM)
    return pl.pallas_call(
        build_kernel,
        out_shape=[jax.ShapeDtypeStruct(s, jnp.bfloat16) for s in shapes],
        in_specs=[hbm] * 3,
        out_specs=[vmem] * len(shapes),
        scratch_shapes=[
            pltpu.SMEM(kernel_rows.shape, jnp.float32),
            pltpu.SMEM(kernel_cols.shape, jnp.float32),
            pltpu.VMEM(kernel_depth.shape, jnp.bfloat16),
            pltpu.VMEM((RADIUS, LANES), jnp.float32),
            pltpu.SemaphoreType.DMA((3,)),
        ],
        compiler_params=pltpu.CompilerParams(vmem_limit_bytes=24 << 20),
        cost_estimate=pl.CostEstimate(flops=30 << 20, bytes_accessed=16 << 20, transcendentals=0),
        name="build",
    )(*[pltpu.with_memory_space_constraint(a, pltpu.HBM) for a in (kernel_rows, kernel_cols, kernel_depth)])


def halves(values):
    high = values.astype(jnp.bfloat16)
    return high, (values - high.astype(jnp.float32)).astype(jnp.bfloat16)


def dot3(left_high, left_low, right_high, right_low):
    left = jnp.concatenate([left_high, left_low, left_high], 1)
    right = jnp.concatenate([right_high, right_high, right_low], 0)
    return jnp.dot(left, right, preferred_element_type=jnp.float32)


def near_kernel(own, north, south, side_a, side_b, wh, wl, out, xh, xl):
    depth = own.shape[-1]
    start = 0
    for ref in (own, north, south, side_a, side_b):
        size = ref.shape[0] * ref.shape[1]
        high, low = halves(ref[...].reshape(size, depth))
        xh[start : start + size] = high
        xl[start : start + size] = low
        start += size

    def density(index, carry):
        rows = pl.ds(pl.multiple_of(index * CELLS, CELLS), CELLS)
        out[rows] = dot3(wh[rows], wl[rows], xh[...], xl[...])
        return carry

    lax.fori_loop(0, DENSITIES, density, 0)


def near(pieces, wh, wl):
    depth = pieces[0].shape[-1]
    keys = 3 * CELLS
    vmem = pl.BlockSpec(memory_space=pltpu.VMEM)
    return pl.pallas_call(
        near_kernel,
        out_shape=jax.ShapeDtypeStruct((DENSITIES * CELLS, depth), jnp.float32),
        in_specs=[vmem] * 7,
        out_specs=vmem,
        scratch_shapes=[pltpu.VMEM((keys, depth), jnp.bfloat16)] * 2,
        compiler_params=pltpu.CompilerParams(vmem_limit_bytes=16 << 20),
        cost_estimate=pl.CostEstimate(
            flops=6 * DENSITIES * CELLS * keys * depth, bytes_accessed=10 << 20, transcendentals=0
        ),
        name="near",
    )(*pieces, wh, wl)


def middle_kernel(
    partial, corner_a, corner_b, wh, wl, bands, bands_t, th, tl, hessian, out_a, out_b, bh, bl,
    xh, xl, dens, low
):
    depth = partial.shape[-1]
    half = CELLS // 2
    for start, ref in ((0, corner_a), (half, corner_b)):
        high, rest = halves(ref[...].reshape(half, depth))
        xh[start : start + half] = high
        xl[start : start + half] = rest
    for b in range(DENSITIES):
        rows = slice(b * CELLS, (b + 1) * CELLS)
        lateral = partial[rows] + dot3(wh[rows], wl[rows], xh[...], xl[...])
        dens[b] = jnp.dot(lateral.astype(jnp.bfloat16), bands[b], preferred_element_type=jnp.float32)
    for a in range(DENSITIES):
        for r in range(TILE):
            cells = slice(r * TILE, (r + 1) * TILE)
            grad = hessian[a, 0, r].astype(jnp.float32) * dens[0, cells]
            for b in range(1, DENSITIES):
                grad = grad + hessian[a, b, r].astype(jnp.float32) * dens[b, cells]
            low[a, cells] = grad.astype(jnp.bfloat16)
        back = jnp.dot(low[a], bands_t[a], preferred_element_type=jnp.float32)
        rows = slice(a * CELLS, (a + 1) * CELLS)
        high, rest = halves(back)
        bh[rows] = high
        bl[rows] = rest
    corners = slice(3 * CELLS, 4 * CELLS)
    total = dot3(th[corners], tl[corners], bh[...], bl[...])
    out_a[...] = total[:half].reshape(out_a.shape)
    out_b[...] = total[half:].reshape(out_b.shape)


def middle(partial, corner_a, corner_b, wh, wl, bands, bands_t, th, tl, hessian):
    depth = partial.shape[-1]
    edge = jax.ShapeDtypeStruct(corner_a.shape, jnp.float32)
    back = jax.ShapeDtypeStruct((DENSITIES * CELLS, depth), jnp.bfloat16)
    vmem = pl.BlockSpec(memory_space=pltpu.VMEM)
    return pl.pallas_call(
        middle_kernel,
        out_shape=[edge, edge, back, back],
        in_specs=[vmem] * 10,
        out_specs=[vmem] * 4,
        scratch_shapes=[
            pltpu.VMEM((CELLS, depth), jnp.bfloat16),
            pltpu.VMEM((CELLS, depth), jnp.bfloat16),
            pltpu.VMEM((DENSITIES, CELLS, depth), jnp.float32),
            pltpu.VMEM((DENSITIES, CELLS, depth), jnp.bfloat16),
        ],
        compiler_params=pltpu.CompilerParams(vmem_limit_bytes=24 << 20),
        cost_estimate=pl.CostEstimate(
            flops=DENSITIES * CELLS * depth * (12 * CELLS + 4 * depth), bytes_accessed=16 << 20, transcendentals=0
        ),
        name="middle",
    )(partial, corner_a, corner_b, wh, wl, bands, bands_t, th, tl, hessian)


def spread_kernel(group, th, tl, bh, bl, *outs):
    rows = slice(group * CELLS, (group + 1) * CELLS)
    total = dot3(th[rows], tl[rows], bh[...], bl[...])
    start = 0
    for out in outs:
        size = out.shape[0] * out.shape[1]
        out[...] = total[start : start + size].reshape(out.shape)
        start += size


def spread(group, th, tl, bh, bl, shapes):
    depth = bh.shape[-1]
    vmem = pl.BlockSpec(memory_space=pltpu.VMEM)
    return pl.pallas_call(
        functools.partial(spread_kernel, group),
        out_shape=[jax.ShapeDtypeStruct(s + (depth,), jnp.float32) for s in shapes],
        in_specs=[vmem] * 4,
        out_specs=[vmem] * len(shapes),
        compiler_params=pltpu.CompilerParams(vmem_limit_bytes=16 << 20),
        cost_estimate=pl.CostEstimate(
            flops=6 * CELLS * th.shape[1] * depth, bytes_accessed=6 << 20, transcendentals=0
        ),
        name="spread",
    )(th, tl, bh, bl)


PIECES = 8


def cut_kernel(tangent, last, first, side_a, side_b, tile, sems):
    right = side_is_right()
    step = TILE // PIECES
    copies = [
        pltpu.make_async_copy(tangent.at[pl.ds(step * i, step)], tile.at[pl.ds(step * i, step)], sems.at[i])
        for i in range(PIECES)
    ]
    for copy in copies:
        copy.start()
    for copy in copies:
        copy.wait()
    cols = lambda place: pl.ds(pl.multiple_of(place * RADIUS, RADIUS), RADIUS)
    last[...] = tile[RADIUS:]
    first[...] = tile[:RADIUS]
    side_a[...] = tile[:, cols(right)]
    side_b[...] = tile[:, cols(1 - right)]


def cut(tangent):
    span_rows, span_cols, depth = tangent.shape
    shapes = [(RADIUS, span_cols)] * 2 + [(span_rows, RADIUS)] * 2 + [(span_rows, span_cols)]
    vmem = pl.BlockSpec(memory_space=pltpu.VMEM)
    return pl.pallas_call(
        cut_kernel,
        out_shape=[jax.ShapeDtypeStruct(s + (depth,), jnp.float32) for s in shapes],
        in_specs=[pl.BlockSpec(memory_space=pltpu.HBM)],
        out_specs=[vmem] * 5,
        scratch_shapes=[pltpu.SemaphoreType.DMA((PIECES,))],
        compiler_params=pltpu.CompilerParams(vmem_limit_bytes=8 << 20),
        cost_estimate=pl.CostEstimate(flops=0, bytes_accessed=3 << 20, transcendentals=0),
        name="cut",
    )(pltpu.with_memory_space_constraint(tangent, pltpu.HBM))


def shift(cells, axis, step):
    count = lax.axis_size(axis)
    return lax.ppermute(cells, axis, [(i, (i + step) % count) for i in range(count)])


def swap_a(cells):
    count = lax.axis_size("gy")
    return lax.ppermute(cells, "gy", [(j, j ^ 1) for j in range(count)])


def swap_b(cells):
    count = lax.axis_size("gy")
    return lax.ppermute(cells, "gy", [(j, (j + (1 if j % 2 else -1)) % count) for j in range(count)])


def swapped(for_b, for_a):
    from_b = swap_b(for_b)
    for_b, for_a = lax.optimization_barrier((for_b, for_a))
    return from_b, swap_a(for_a)


def per_device(tangent, hessian, kernel_rows, kernel_cols, kernel_depth):
    span_rows, span_cols, depth = tangent.shape
    reach = RADIUS
    right = side_is_right()

    def side_cols(cells, place):
        return jnp.where(place == 1, cells[:, reach:], cells[:, :reach])

    def joined(from_a, from_b):
        left, other = jnp.concatenate([from_a, from_b], 1), jnp.concatenate([from_b, from_a], 1)
        return jnp.where(right == 1, other, left)

    last, first, cols_a, cols_b, tile = cut(tangent)
    north = shift(last, "gx", 1)
    south = shift(first, "gx", -1)
    side_b, side_a = swapped(cols_b, cols_a)

    nh, nl, ch, cl, th, tl, bands, bands_t = build(kernel_rows, kernel_cols, kernel_depth, depth)

    sides = jnp.concatenate([north, south], 0)
    corner_b, corner_a = swapped(side_cols(sides, 1 - right), side_cols(sides, right))

    partial = near((tile, north, south, side_a, side_b), nh, nl)
    to_a, to_b, bh, bl = middle(partial, corner_a, corner_b, ch, cl, bands, bands_t, th, tl, hessian)
    from_b, from_a = swapped(to_b, to_a)

    edge_a, edge_b = spread(2, th, tl, bh, bl, [(span_rows, reach)] * 2)
    edge_from_b, edge_from_a = swapped(edge_b, edge_a)

    (around,) = spread(1, th, tl, bh, bl, [(span_rows, span_cols)])
    around = around + joined(from_a, from_b)
    above, below = around[:reach], around[reach:]
    side_from_n = shift(below, "gx", 1)
    above, below = lax.optimization_barrier((above, below))
    side_from_s = shift(above, "gx", -1)

    around, bh, bl = lax.optimization_barrier((around, bh, bl))
    (own,) = spread(0, th, tl, bh, bl, [(span_rows, span_cols)])
    own = lax.optimization_barrier(own + joined(edge_from_a, edge_from_b))
    return own + jnp.concatenate([side_from_n, side_from_s], 0)


def solution(mesh):
    return jax.shard_map(
        per_device,
        mesh=mesh,
        in_specs=(P("gx", "gy", None), P(None, None, "gx", "gy", None), P(), P(), P()),
        out_specs=P("gx", "gy", None),
        check_vma=False,
    )
```

```python
import functools

import jax
import jax.numpy as jnp
from jax import lax
from jax.experimental import pallas as pl
from jax.experimental.pallas import tpu as pltpu
from jax.sharding import PartitionSpec as P

RADIUS = 8
DENSITIES = 5
TAPS = 2 * RADIUS + 1
TILE = 16
CELLS = TILE * TILE


LANES = 128
TURN = TILE + RADIUS


def side_is_right():
    return 1 - lax.rem(lax.axis_index("gy"), 2)


def taps_at(weights, density, offsets):
    total = jnp.zeros(offsets.shape, jnp.float32)
    for tap in range(TAPS):
        total = jnp.where(offsets == tap - RADIUS, weights[density, tap], total)
    return total


def taps_of_all(weights, offsets):
    totals = [jnp.zeros(offsets.shape, jnp.float32)] * DENSITIES
    for tap in range(TAPS):
        here = offsets == tap - RADIUS
        totals = [jnp.where(here, weights[a, tap], totals[a]) for a in range(DENSITIES)]
    return totals


def build_kernel(
    kr_hbm, kc_hbm, kd_hbm, nh, nl, ch, cl, th, tl, bands, bands_t, kr, kc, depth_taps, depth_row, sems
):
    copies = [
        pltpu.make_async_copy(kr_hbm, kr, sems.at[0]),
        pltpu.make_async_copy(kc_hbm, kc, sems.at[1]),
        pltpu.make_async_copy(kd_hbm, depth_taps, sems.at[2]),
    ]
    for copy in copies:
        copy.start()
    copies[2].wait()
    right = side_is_right()
    iota = lambda shape, dim: lax.broadcasted_iota(jnp.int32, shape, dim)

    depth_row[...] = jnp.zeros(depth_row.shape, jnp.float32)
    depth_row[:DENSITIES, :TAPS] = depth_taps[...].astype(jnp.float32)
    depth = bands.shape[-1]
    block = (LANES, LANES)
    ahead = iota(block, 1) - iota(block, 0)

    def band(density, carry):
        row = jnp.broadcast_to(depth_row[pl.ds(density, 1)], block)
        ring_t = pltpu.roll(row, LANES - RADIUS, 1, stride=1, stride_axis=0)
        for ref, ring in ((bands_t, ring_t), (bands, ring_t.T)):
            ref[density] = jnp.zeros((depth, depth), jnp.bfloat16)
            for step in (-1, 0, 1):
                here = jnp.abs(ahead + step * LANES) <= RADIUS
                part = jnp.where(here, ring, 0.0).astype(jnp.bfloat16)
                for start in range(0, depth, LANES):
                    across = start + step * LANES
                    if 0 <= across < depth:
                        ref[density, start : start + LANES, across : across + LANES] = part
        return carry

    lax.fori_loop(0, DENSITIES, band, 0)
    for copy in copies[:2]:
        copy.wait()

    def put(high_ref, low_ref, start, lanes, values):
        high, low = halves(values)
        high_ref[start : start + TILE, lanes] = high
        low_ref[start : start + TILE, lanes] = low

    def forward(high_ref, low_ref, first):
        def chunk(index, carry):
            lanes = pl.ds(pl.multiple_of(index * LANES, LANES), LANES)
            group, half = (first + index) // 2, (first + index) % 2
            lane, tile_place = iota((TILE, LANES), 1), iota((TILE, LANES), 0)
            wide, slim = lane >> 4, lane >> 3
            row = jnp.where(group == 2, slim, jnp.where(slim < RADIUS, slim - RADIUS, slim + RADIUS))
            row = jnp.where(group == 1, wide - RADIUS + TURN * half, row)
            row = jnp.where(group == 0, wide + RADIUS * half, row)
            side = half + right - 2 * half * right
            col = jnp.where(group < 2, lane & 15, (lane & 7) - RADIUS + TURN * side)
            by_row = taps_of_all(kr, row - tile_place)
            by_col = taps_of_all(kc, col - tile_place)
            for a in range(DENSITIES):
                for r in range(TILE):
                    put(high_ref, low_ref, a * CELLS + r * TILE, lanes, by_row[a][r : r + 1] * by_col[a])
            return carry

        lax.fori_loop(0, high_ref.shape[1] // LANES, chunk, 0)

    forward(nh, nl, 0)
    forward(ch, cl, 6)

    def transposes(index, carry):
        density, half = index // 2, index % 2
        lanes = pl.ds(pl.multiple_of(index * LANES, LANES), LANES)
        shape = (TILE + 2 * RADIUS, LANES)
        place, lane = iota(shape, 0), iota(shape, 1)
        turn = TURN * right
        turned = place - RADIUS + jnp.where(place < RADIUS, turn, jnp.where(place < TILE + RADIUS, 0, -turn))
        by_row = taps_at(kr, density, place - RADIUS - (lane >> 4) - RADIUS * half)
        by_col = taps_at(kc, density, turned - (lane & 15))
        row = lambda r: by_row[r + RADIUS : r + RADIUS + 1]
        inner = list(range(TILE))
        outer = list(range(-RADIUS, 0)) + list(range(TILE, TILE + RADIUS))
        mid = by_col[RADIUS : RADIUS + TILE]
        for place, r in enumerate(inner + outer):
            put(th, tl, place * TILE, lanes, row(r) * mid)
        for base, rows in ((2 * CELLS, inner), (3 * CELLS, outer)):
            for side, edge in enumerate((by_col[:RADIUS], by_col[RADIUS + TILE :])):
                for pair in range(TILE // 2):
                    both = [row(rows[2 * pair]) * edge, row(rows[2 * pair + 1]) * edge]
                    put(th, tl, base + side * CELLS // 2 + pair * TILE, lanes, jnp.concatenate(both, 0))
        return carry

    lax.fori_loop(0, DENSITIES * CELLS // LANES, transposes, 0)

def build(kernel_rows, kernel_cols, kernel_depth, depth):
    cells = DENSITIES * CELLS
    shapes = [(cells, 3 * CELLS)] * 2 + [(cells, CELLS)] * 2
    shapes += [(4 * CELLS, cells)] * 2
    shapes += [(DENSITIES, depth, depth)] * 2
    vmem = pl.BlockSpec(memory_space=pltpu.VMEM)
    hbm = pl.BlockSpec(memory_space=pltpu.HBM)
    return pl.pallas_call(
        build_kernel,
        out_shape=[jax.ShapeDtypeStruct(s, jnp.bfloat16) for s in shapes],
        in_specs=[hbm] * 3,
        out_specs=[vmem] * len(shapes),
        scratch_shapes=[
            pltpu.SMEM(kernel_rows.shape, jnp.float32),
            pltpu.SMEM(kernel_cols.shape, jnp.float32),
            pltpu.VMEM(kernel_depth.shape, jnp.bfloat16),
            pltpu.VMEM((RADIUS, LANES), jnp.float32),
            pltpu.SemaphoreType.DMA((3,)),
        ],
        compiler_params=pltpu.CompilerParams(vmem_limit_bytes=24 << 20),
        cost_estimate=pl.CostEstimate(flops=30 << 20, bytes_accessed=16 << 20, transcendentals=0),
        name="build",
    )(*[pltpu.with_memory_space_constraint(a, pltpu.HBM) for a in (kernel_rows, kernel_cols, kernel_depth)])


def halves(values):
    high = values.astype(jnp.bfloat16)
    return high, (values - high.astype(jnp.float32)).astype(jnp.bfloat16)


def dot3(left_high, left_low, right_high, right_low):
    left = jnp.concatenate([left_high, left_low, left_high], 1)
    right = jnp.concatenate([right_high, right_high, right_low], 0)
    return jnp.dot(left, right, preferred_element_type=jnp.float32)


def near_kernel(own, north, south, side_a, side_b, wh, wl, out, xh, xl):
    depth = own.shape[-1]
    start = 0
    for ref in (own, north, south, side_a, side_b):
        size = ref.shape[0] * ref.shape[1]
        high, low = halves(ref[...].reshape(size, depth))
        xh[start : start + size] = high
        xl[start : start + size] = low
        start += size

    def density(index, carry):
        rows = pl.ds(pl.multiple_of(index * CELLS, CELLS), CELLS)
        out[rows] = dot3(wh[rows], wl[rows], xh[...], xl[...])
        return carry

    lax.fori_loop(0, DENSITIES, density, 0)


def near(pieces, wh, wl):
    depth = pieces[0].shape[-1]
    keys = 3 * CELLS
    vmem = pl.BlockSpec(memory_space=pltpu.VMEM)
    return pl.pallas_call(
        near_kernel,
        out_shape=jax.ShapeDtypeStruct((DENSITIES * CELLS, depth), jnp.float32),
        in_specs=[vmem] * 7,
        out_specs=vmem,
        scratch_shapes=[pltpu.VMEM((keys, depth), jnp.bfloat16)] * 2,
        compiler_params=pltpu.CompilerParams(vmem_limit_bytes=16 << 20),
        cost_estimate=pl.CostEstimate(
            flops=6 * DENSITIES * CELLS * keys * depth, bytes_accessed=10 << 20, transcendentals=0
        ),
        name="near",
    )(*pieces, wh, wl)


def middle_kernel(
    partial, corner_a, corner_b, wh, wl, bands, bands_t, th, tl, hessian, out_a, out_b, bh, bl,
    xh, xl, dens, low
):
    depth = partial.shape[-1]
    half = CELLS // 2
    for start, ref in ((0, corner_a), (half, corner_b)):
        high, rest = halves(ref[...].reshape(half, depth))
        xh[start : start + half] = high
        xl[start : start + half] = rest
    for b in range(DENSITIES):
        rows = slice(b * CELLS, (b + 1) * CELLS)
        lateral = partial[rows] + dot3(wh[rows], wl[rows], xh[...], xl[...])
        dens[b] = jnp.dot(lateral.astype(jnp.bfloat16), bands[b], preferred_element_type=jnp.float32)
    for a in range(DENSITIES):
        for r in range(TILE):
            cells = slice(r * TILE, (r + 1) * TILE)
            grad = hessian[a, 0, r].astype(jnp.float32) * dens[0, cells]
            for b in range(1, DENSITIES):
                grad = grad + hessian[a, b, r].astype(jnp.float32) * dens[b, cells]
            low[a, cells] = grad.astype(jnp.bfloat16)
        back = jnp.dot(low[a], bands_t[a], preferred_element_type=jnp.float32)
        rows = slice(a * CELLS, (a + 1) * CELLS)
        high, rest = halves(back)
        bh[rows] = high
        bl[rows] = rest
    corners = slice(3 * CELLS, 4 * CELLS)
    total = dot3(th[corners], tl[corners], bh[...], bl[...])
    out_a[...] = total[:half].reshape(out_a.shape)
    out_b[...] = total[half:].reshape(out_b.shape)


def middle(partial, corner_a, corner_b, wh, wl, bands, bands_t, th, tl, hessian):
    depth = partial.shape[-1]
    edge = jax.ShapeDtypeStruct(corner_a.shape, jnp.float32)
    back = jax.ShapeDtypeStruct((DENSITIES * CELLS, depth), jnp.bfloat16)
    vmem = pl.BlockSpec(memory_space=pltpu.VMEM)
    return pl.pallas_call(
        middle_kernel,
        out_shape=[edge, edge, back, back],
        in_specs=[vmem] * 10,
        out_specs=[vmem] * 4,
        scratch_shapes=[
            pltpu.VMEM((CELLS, depth), jnp.bfloat16),
            pltpu.VMEM((CELLS, depth), jnp.bfloat16),
            pltpu.VMEM((DENSITIES, CELLS, depth), jnp.float32),
            pltpu.VMEM((DENSITIES, CELLS, depth), jnp.bfloat16),
        ],
        compiler_params=pltpu.CompilerParams(vmem_limit_bytes=24 << 20),
        cost_estimate=pl.CostEstimate(
            flops=DENSITIES * CELLS * depth * (12 * CELLS + 4 * depth), bytes_accessed=16 << 20, transcendentals=0
        ),
        name="middle",
    )(partial, corner_a, corner_b, wh, wl, bands, bands_t, th, tl, hessian)


def spread_kernel(group, th, tl, bh, bl, *outs):
    rows = slice(group * CELLS, (group + 1) * CELLS)
    total = dot3(th[rows], tl[rows], bh[...], bl[...])
    start = 0
    for out in outs:
        size = out.shape[0] * out.shape[1]
        out[...] = total[start : start + size].reshape(out.shape)
        start += size


def spread(group, th, tl, bh, bl, shapes):
    depth = bh.shape[-1]
    vmem = pl.BlockSpec(memory_space=pltpu.VMEM)
    return pl.pallas_call(
        functools.partial(spread_kernel, group),
        out_shape=[jax.ShapeDtypeStruct(s + (depth,), jnp.float32) for s in shapes],
        in_specs=[vmem] * 4,
        out_specs=[vmem] * len(shapes),
        compiler_params=pltpu.CompilerParams(vmem_limit_bytes=16 << 20),
        cost_estimate=pl.CostEstimate(
            flops=6 * CELLS * th.shape[1] * depth, bytes_accessed=6 << 20, transcendentals=0
        ),
        name="spread",
    )(th, tl, bh, bl)


PIECES = 8


def cut_kernel(tangent, last, first, side_a, side_b, tile, sems):
    right = side_is_right()
    step = TILE // PIECES
    copies = [
        pltpu.make_async_copy(tangent.at[pl.ds(step * i, step)], tile.at[pl.ds(step * i, step)], sems.at[i])
        for i in range(PIECES)
    ]
    for copy in copies:
        copy.start()
    for copy in copies:
        copy.wait()
    cols = lambda place: pl.ds(pl.multiple_of(place * RADIUS, RADIUS), RADIUS)
    last[...] = tile[RADIUS:]
    first[...] = tile[:RADIUS]
    side_a[...] = tile[:, cols(right)]
    side_b[...] = tile[:, cols(1 - right)]


def cut(tangent):
    span_rows, span_cols, depth = tangent.shape
    shapes = [(RADIUS, span_cols)] * 2 + [(span_rows, RADIUS)] * 2 + [(span_rows, span_cols)]
    vmem = pl.BlockSpec(memory_space=pltpu.VMEM)
    return pl.pallas_call(
        cut_kernel,
        out_shape=[jax.ShapeDtypeStruct(s + (depth,), jnp.float32) for s in shapes],
        in_specs=[pl.BlockSpec(memory_space=pltpu.HBM)],
        out_specs=[vmem] * 5,
        scratch_shapes=[pltpu.SemaphoreType.DMA((PIECES,))],
        compiler_params=pltpu.CompilerParams(vmem_limit_bytes=8 << 20),
        cost_estimate=pl.CostEstimate(flops=0, bytes_accessed=3 << 20, transcendentals=0),
        name="cut",
    )(pltpu.with_memory_space_constraint(tangent, pltpu.HBM))


def shift(cells, axis, step):
    count = lax.axis_size(axis)
    return lax.ppermute(cells, axis, [(i, (i + step) % count) for i in range(count)])


def swap_a(cells):
    count = lax.axis_size("gy")
    return lax.ppermute(cells, "gy", [(j, j ^ 1) for j in range(count)])


def swap_b(cells):
    count = lax.axis_size("gy")
    return lax.ppermute(cells, "gy", [(j, (j + (1 if j % 2 else -1)) % count) for j in range(count)])


RUN = 8


def b_place(j, count):
    return (j + (1 if j % 2 else -1)) % count


def over_both(cells, chosen):
    rows, cols = lax.axis_size("gx"), lax.axis_size("gy")
    pairs = [
        (i * cols + j, (i + chosen(i)) % rows * cols + b_place(j, cols))
        for i in range(rows)
        for j in range(cols)
        if chosen(i) is not None
    ]
    return lax.ppermute(cells, ("gx", "gy"), pairs)


def swap_b_within(cells):
    return over_both(cells, lambda i: None if i % RUN in (0, RUN - 1) else 0)


def over_wrap(cells):
    return over_both(cells, lambda i: {0: -1, RUN - 1: 1}.get(i % RUN))


def to_ends(cells):
    return over_both(cells, lambda i: {1: -1, RUN - 2: 1}.get(i % RUN))


def from_ends(cells):
    return over_both(cells, lambda i: {0: 1, RUN - 1: -1}.get(i % RUN))


def swapped(for_b, for_a):
    from_b = swap_b(for_b)
    for_b, for_a = lax.optimization_barrier((for_b, for_a))
    return from_b, swap_a(for_a)


def per_device(tangent, hessian, kernel_rows, kernel_cols, kernel_depth):
    span_rows, span_cols, depth = tangent.shape
    reach = RADIUS
    right = side_is_right()

    def side_cols(cells, place):
        return jnp.where(place == 1, cells[:, reach:], cells[:, :reach])

    def joined(from_a, from_b):
        left, other = jnp.concatenate([from_a, from_b], 1), jnp.concatenate([from_b, from_a], 1)
        return jnp.where(right == 1, other, left)

    last, first, cols_a, cols_b, tile = cut(tangent)
    north = shift(last, "gx", 1)
    south = shift(first, "gx", -1)
    side_b, side_a = swapped(cols_b, cols_a)
    lower = lax.rem(lax.axis_index("gx"), RUN) >= RUN // 2
    facing = jnp.where(lower, cols_b[reach:], cols_b[:reach])
    beyond, within = over_wrap(facing), to_ends(facing)

    nh, nl, ch, cl, th, tl, bands, bands_t = build(kernel_rows, kernel_cols, kernel_depth, depth)

    sides = jnp.concatenate([north, south], 0)
    corner_b = swap_b_within(side_cols(sides, 1 - right))
    corner_a = swap_a(side_cols(sides, right))
    direct = jnp.where(lower, jnp.concatenate([within, beyond], 0), jnp.concatenate([beyond, within], 0))
    corner_b = corner_b + direct

    partial = near((tile, north, south, side_a, side_b), nh, nl)
    to_a, to_b, bh, bl = middle(partial, corner_a, corner_b, ch, cl, bands, bands_t, th, tl, hessian)
    from_b, from_a = swap_b_within(to_b), swap_a(to_a)

    edge_a, edge_b = spread(2, th, tl, bh, bl, [(span_rows, reach)] * 2)
    edge_from_b, edge_from_a = swapped(edge_b, edge_a)
    beyond = over_wrap(jnp.where(lower, to_b[reach:], to_b[:reach]))
    within = from_ends(jnp.where(lower, to_b[:reach], to_b[reach:]))

    (around,) = spread(1, th, tl, bh, bl, [(span_rows, span_cols)])
    around = around + joined(from_a, from_b)
    above, below = around[:reach], around[reach:]
    side_from_n = shift(below, "gx", 1)
    above, below = lax.optimization_barrier((above, below))
    side_from_s = shift(above, "gx", -1)

    around, bh, bl = lax.optimization_barrier((around, bh, bl))
    (own,) = spread(0, th, tl, bh, bl, [(span_rows, span_cols)])
    direct = beyond + within
    blank = jnp.zeros_like(direct)
    direct = jnp.where(lower, jnp.concatenate([blank, direct], 0), jnp.concatenate([direct, blank], 0))
    own = lax.optimization_barrier(own + joined(edge_from_a, edge_from_b + direct))
    return own + jnp.concatenate([side_from_n, side_from_s], 0)


def solution(mesh):
    return jax.shard_map(
        per_device,
        mesh=mesh,
        in_specs=(P("gx", "gy", None), P(None, None, "gx", "gy", None), P(), P(), P()),
        out_specs=P("gx", "gy", None),
        check_vma=False,
    )
```

```python
import functools

import jax
import jax.numpy as jnp
from jax import lax
from jax.experimental import pallas as pl
from jax.experimental.pallas import tpu as pltpu
from jax.sharding import PartitionSpec as P

RADIUS = 8
DENSITIES = 5
TAPS = 2 * RADIUS + 1
TILE = 16
CELLS = TILE * TILE


LANES = 128
TURN = TILE + RADIUS


def side_is_right():
    return 1 - lax.rem(lax.axis_index("gy"), 2)


def taps_at(weights, density, offsets):
    total = jnp.zeros(offsets.shape, jnp.float32)
    for tap in range(TAPS):
        total = jnp.where(offsets == tap - RADIUS, weights[density, tap], total)
    return total


def taps_of_all(weights, offsets):
    totals = [jnp.zeros(offsets.shape, jnp.float32)] * DENSITIES
    for tap in range(TAPS):
        here = offsets == tap - RADIUS
        totals = [jnp.where(here, weights[a, tap], totals[a]) for a in range(DENSITIES)]
    return totals


def build_kernel(
    kr_hbm, kc_hbm, kd_hbm, nh, nl, ch, cl, th, tl, bands, bands_t, kr, kc, depth_taps, depth_row, sems
):
    copies = [
        pltpu.make_async_copy(kr_hbm, kr, sems.at[0]),
        pltpu.make_async_copy(kc_hbm, kc, sems.at[1]),
        pltpu.make_async_copy(kd_hbm, depth_taps, sems.at[2]),
    ]
    for copy in copies:
        copy.start()
    copies[2].wait()
    right = side_is_right()
    iota = lambda shape, dim: lax.broadcasted_iota(jnp.int32, shape, dim)

    depth_row[...] = jnp.zeros(depth_row.shape, jnp.float32)
    depth_row[:DENSITIES, :TAPS] = depth_taps[...].astype(jnp.float32)
    depth = bands.shape[-1]
    block = (LANES, LANES)
    ahead = iota(block, 1) - iota(block, 0)

    def band(density, carry):
        row = jnp.broadcast_to(depth_row[pl.ds(density, 1)], block)
        ring_t = pltpu.roll(row, LANES - RADIUS, 1, stride=1, stride_axis=0)
        for ref, ring in ((bands_t, ring_t), (bands, ring_t.T)):
            ref[density] = jnp.zeros((depth, depth), jnp.bfloat16)
            for step in (-1, 0, 1):
                here = jnp.abs(ahead + step * LANES) <= RADIUS
                part = jnp.where(here, ring, 0.0).astype(jnp.bfloat16)
                for start in range(0, depth, LANES):
                    across = start + step * LANES
                    if 0 <= across < depth:
                        ref[density, start : start + LANES, across : across + LANES] = part
        return carry

    lax.fori_loop(0, DENSITIES, band, 0)
    for copy in copies[:2]:
        copy.wait()

    def put(high_ref, low_ref, start, lanes, values):
        high, low = halves(values)
        high_ref[start : start + TILE, lanes] = high
        low_ref[start : start + TILE, lanes] = low

    def forward(high_ref, low_ref, first):
        def chunk(index, carry):
            lanes = pl.ds(pl.multiple_of(index * LANES, LANES), LANES)
            group, half = (first + index) // 2, (first + index) % 2
            lane, tile_place = iota((TILE, LANES), 1), iota((TILE, LANES), 0)
            wide, slim = lane >> 4, lane >> 3
            row = jnp.where(group == 1, wide - RADIUS + TURN * half, slim)
            row = jnp.where(group == 0, wide + RADIUS * half, row)
            row = jnp.where(group == 3, (slim & 7) - RADIUS + TURN * half, row)
            side = jnp.where(group == 3, lane >> 6, half)
            side = side + right - 2 * side * right
            col = jnp.where(group < 2, lane & 15, (lane & 7) - RADIUS + TURN * side)
            by_row = taps_of_all(kr, row - tile_place)
            by_col = taps_of_all(kc, col - tile_place)
            for a in range(DENSITIES):
                for r in range(TILE):
                    put(high_ref, low_ref, a * CELLS + r * TILE, lanes, by_row[a][r : r + 1] * by_col[a])
            return carry

        lax.fori_loop(0, high_ref.shape[1] // LANES, chunk, 0)

    forward(nh, nl, 0)
    forward(ch, cl, 6)

    def transposes(index, carry):
        density, half = index // 2, index % 2
        lanes = pl.ds(pl.multiple_of(index * LANES, LANES), LANES)
        shape = (TILE + 2 * RADIUS, LANES)
        place, lane = iota(shape, 0), iota(shape, 1)
        turn = TURN * right
        turned = place - RADIUS + jnp.where(place < RADIUS, turn, jnp.where(place < TILE + RADIUS, 0, -turn))
        by_row = taps_at(kr, density, place - RADIUS - (lane >> 4) - RADIUS * half)
        by_col = taps_at(kc, density, turned - (lane & 15))
        row = lambda r: by_row[r + RADIUS : r + RADIUS + 1]
        inner = list(range(TILE))
        outer = list(range(-RADIUS, 0)) + list(range(TILE, TILE + RADIUS))
        mid = by_col[RADIUS : RADIUS + TILE]
        for place, r in enumerate(inner + outer):
            put(th, tl, place * TILE, lanes, row(r) * mid)
        for base, rows in ((2 * CELLS, inner), (3 * CELLS, outer)):
            for side, edge in enumerate((by_col[:RADIUS], by_col[RADIUS + TILE :])):
                for pair in range(TILE // 2):
                    both = [row(rows[2 * pair]) * edge, row(rows[2 * pair + 1]) * edge]
                    put(th, tl, base + side * CELLS // 2 + pair * TILE, lanes, jnp.concatenate(both, 0))
        return carry

    lax.fori_loop(0, DENSITIES * CELLS // LANES, transposes, 0)

def build(kernel_rows, kernel_cols, kernel_depth, depth):
    cells = DENSITIES * CELLS
    shapes = [(cells, 3 * CELLS)] * 2 + [(cells, CELLS)] * 2
    shapes += [(4 * CELLS, cells)] * 2
    shapes += [(DENSITIES, depth, depth)] * 2
    vmem = pl.BlockSpec(memory_space=pltpu.VMEM)
    hbm = pl.BlockSpec(memory_space=pltpu.HBM)
    return pl.pallas_call(
        build_kernel,
        out_shape=[jax.ShapeDtypeStruct(s, jnp.bfloat16) for s in shapes],
        in_specs=[hbm] * 3,
        out_specs=[vmem] * len(shapes),
        scratch_shapes=[
            pltpu.SMEM(kernel_rows.shape, jnp.float32),
            pltpu.SMEM(kernel_cols.shape, jnp.float32),
            pltpu.VMEM(kernel_depth.shape, jnp.bfloat16),
            pltpu.VMEM((RADIUS, LANES), jnp.float32),
            pltpu.SemaphoreType.DMA((3,)),
        ],
        compiler_params=pltpu.CompilerParams(vmem_limit_bytes=24 << 20),
        cost_estimate=pl.CostEstimate(flops=30 << 20, bytes_accessed=16 << 20, transcendentals=0),
        name="build",
    )(*[pltpu.with_memory_space_constraint(a, pltpu.HBM) for a in (kernel_rows, kernel_cols, kernel_depth)])


def halves(values):
    high = values.astype(jnp.bfloat16)
    return high, (values - high.astype(jnp.float32)).astype(jnp.bfloat16)


def dot3(left_high, left_low, right_high, right_low):
    left = jnp.concatenate([left_high, left_low, left_high], 1)
    right = jnp.concatenate([right_high, right_high, right_low], 0)
    return jnp.dot(left, right, preferred_element_type=jnp.float32)


def near_kernel(own, north, south, side_a, side_b, wh, wl, out, xh, xl):
    depth = own.shape[-1]
    start = 0
    for ref in (own, north, south, side_a, side_b):
        size = ref.shape[0] * ref.shape[1]
        high, low = halves(ref[...].reshape(size, depth))
        xh[start : start + size] = high
        xl[start : start + size] = low
        start += size

    def density(index, carry):
        rows = pl.ds(pl.multiple_of(index * CELLS, CELLS), CELLS)
        out[rows] = dot3(wh[rows], wl[rows], xh[...], xl[...])
        return carry

    lax.fori_loop(0, DENSITIES, density, 0)


def near(pieces, wh, wl):
    depth = pieces[0].shape[-1]
    keys = 3 * CELLS
    vmem = pl.BlockSpec(memory_space=pltpu.VMEM)
    return pl.pallas_call(
        near_kernel,
        out_shape=jax.ShapeDtypeStruct((DENSITIES * CELLS, depth), jnp.float32),
        in_specs=[vmem] * 7,
        out_specs=vmem,
        scratch_shapes=[pltpu.VMEM((keys, depth), jnp.bfloat16)] * 2,
        compiler_params=pltpu.CompilerParams(vmem_limit_bytes=16 << 20),
        cost_estimate=pl.CostEstimate(
            flops=6 * DENSITIES * CELLS * keys * depth, bytes_accessed=10 << 20, transcendentals=0
        ),
        name="near",
    )(*pieces, wh, wl)


def middle_kernel(
    partial, corner_a, corner_b, wh, wl, bands, bands_t, th, tl, hessian, out_a, out_b, bh, bl,
    dens, low
):
    depth = partial.shape[-1]
    half = CELLS // 2
    terms = []
    for part in range(2):
        pieces = [ref[part * RADIUS : (part + 1) * RADIUS].reshape(half // 2, depth) for ref in (corner_a, corner_b)]
        high, rest = halves(jnp.concatenate(pieces, 0))
        lanes = slice(part * half, (part + 1) * half)
        tile_rows = [slice(b * CELLS + part * half, b * CELLS + (part + 1) * half) for b in range(DENSITIES)]
        of_all = lambda ref: jnp.concatenate([ref[rows, lanes] for rows in tile_rows], 0)
        terms.append(dot3(of_all(wh), of_all(wl), high, rest))
    for b in range(DENSITIES):
        rows = slice(b * CELLS, (b + 1) * CELLS)
        own = slice(b * half, (b + 1) * half)
        lateral = partial[rows] + jnp.concatenate([terms[0][own], terms[1][own]], 0)
        dens[b] = jnp.dot(lateral.astype(jnp.bfloat16), bands[b], preferred_element_type=jnp.float32)
    for a in range(DENSITIES):
        for r in range(TILE):
            cells = slice(r * TILE, (r + 1) * TILE)
            grad = hessian[a, 0, r].astype(jnp.float32) * dens[0, cells]
            for b in range(1, DENSITIES):
                grad = grad + hessian[a, b, r].astype(jnp.float32) * dens[b, cells]
            low[a, cells] = grad.astype(jnp.bfloat16)
        back = jnp.dot(low[a], bands_t[a], preferred_element_type=jnp.float32)
        rows = slice(a * CELLS, (a + 1) * CELLS)
        high, rest = halves(back)
        bh[rows] = high
        bl[rows] = rest
    corners = slice(3 * CELLS, 4 * CELLS)
    total = dot3(th[corners], tl[corners], bh[...], bl[...])
    out_a[...] = total[:half].reshape(out_a.shape)
    out_b[...] = total[half:].reshape(out_b.shape)


def middle(partial, corner_a, corner_b, wh, wl, bands, bands_t, th, tl, hessian):
    depth = partial.shape[-1]
    edge = jax.ShapeDtypeStruct(corner_a.shape, jnp.float32)
    back = jax.ShapeDtypeStruct((DENSITIES * CELLS, depth), jnp.bfloat16)
    vmem = pl.BlockSpec(memory_space=pltpu.VMEM)
    return pl.pallas_call(
        middle_kernel,
        out_shape=[edge, edge, back, back],
        in_specs=[vmem] * 10,
        out_specs=[vmem] * 4,
        scratch_shapes=[
            pltpu.VMEM((DENSITIES, CELLS, depth), jnp.float32),
            pltpu.VMEM((DENSITIES, CELLS, depth), jnp.bfloat16),
        ],
        compiler_params=pltpu.CompilerParams(vmem_limit_bytes=24 << 20),
        cost_estimate=pl.CostEstimate(
            flops=DENSITIES * CELLS * depth * (12 * CELLS + 4 * depth), bytes_accessed=16 << 20, transcendentals=0
        ),
        name="middle",
    )(partial, corner_a, corner_b, wh, wl, bands, bands_t, th, tl, hessian)


def spread_kernel(group, th, tl, bh, bl, *outs):
    start = group * CELLS
    for first in range(0, len(outs), 2):
        pair = outs[first : first + 2]
        sizes = [out.shape[0] * out.shape[1] for out in pair]
        total = dot3(th[start : start + sum(sizes)], tl[start : start + sum(sizes)], bh[...], bl[...])
        start += sum(sizes)
        for out, size, offset in zip(pair, sizes, (0, sizes[0])):
            out[...] = total[offset : offset + size].reshape(out.shape)


def spread(group, th, tl, bh, bl, shapes):
    depth = bh.shape[-1]
    vmem = pl.BlockSpec(memory_space=pltpu.VMEM)
    return pl.pallas_call(
        functools.partial(spread_kernel, group),
        out_shape=[jax.ShapeDtypeStruct(s + (depth,), jnp.float32) for s in shapes],
        in_specs=[vmem] * 4,
        out_specs=[vmem] * len(shapes),
        compiler_params=pltpu.CompilerParams(vmem_limit_bytes=16 << 20),
        cost_estimate=pl.CostEstimate(
            flops=6 * sum(r * c for r, c in shapes) * th.shape[1] * depth, bytes_accessed=6 << 20, transcendentals=0
        ),
        name="spread",
    )(th, tl, bh, bl)


PIECES = 8


def cut_kernel(tangent, last, first, side_a, side_b, tile, sems):
    right = side_is_right()
    step = TILE // PIECES
    copies = [
        pltpu.make_async_copy(tangent.at[pl.ds(step * i, step)], tile.at[pl.ds(step * i, step)], sems.at[i])
        for i in range(PIECES)
    ]
    for copy in copies:
        copy.start()
    for copy in copies:
        copy.wait()
    cols = lambda place: pl.ds(pl.multiple_of(place * RADIUS, RADIUS), RADIUS)
    last[...] = tile[RADIUS:]
    first[...] = tile[:RADIUS]
    side_a[...] = tile[:, cols(right)]
    side_b[...] = tile[:, cols(1 - right)]


def cut(tangent):
    span_rows, span_cols, depth = tangent.shape
    shapes = [(RADIUS, span_cols)] * 2 + [(span_rows, RADIUS)] * 2 + [(span_rows, span_cols)]
    vmem = pl.BlockSpec(memory_space=pltpu.VMEM)
    return pl.pallas_call(
        cut_kernel,
        out_shape=[jax.ShapeDtypeStruct(s + (depth,), jnp.float32) for s in shapes],
        in_specs=[pl.BlockSpec(memory_space=pltpu.HBM)],
        out_specs=[vmem] * 5,
        scratch_shapes=[pltpu.SemaphoreType.DMA((PIECES,))],
        compiler_params=pltpu.CompilerParams(vmem_limit_bytes=8 << 20),
        cost_estimate=pl.CostEstimate(flops=0, bytes_accessed=3 << 20, transcendentals=0),
        name="cut",
    )(pltpu.with_memory_space_constraint(tangent, pltpu.HBM))


def shift(cells, axis, step):
    count = lax.axis_size(axis)
    return lax.ppermute(cells, axis, [(i, (i + step) % count) for i in range(count)])


def swap_a(cells):
    count = lax.axis_size("gy")
    return lax.ppermute(cells, "gy", [(j, j ^ 1) for j in range(count)])


def swap_b(cells):
    count = lax.axis_size("gy")
    return lax.ppermute(cells, "gy", [(j, (j + (1 if j % 2 else -1)) % count) for j in range(count)])


def swapped(for_b, for_a):
    from_b = swap_b(for_b)
    for_b, for_a = lax.optimization_barrier((for_b, for_a))
    return from_b, swap_a(for_a)


def per_device(tangent, hessian, kernel_rows, kernel_cols, kernel_depth):
    span_rows, span_cols, depth = tangent.shape
    reach = RADIUS
    right = side_is_right()

    def side_cols(cells, place):
        return jnp.where(place == 1, cells[:, reach:], cells[:, :reach])

    def joined(from_a, from_b):
        left, other = jnp.concatenate([from_a, from_b], 1), jnp.concatenate([from_b, from_a], 1)
        return jnp.where(right == 1, other, left)

    last, first, cols_a, cols_b, tile = cut(tangent)
    north = shift(last, "gx", 1)
    south = shift(first, "gx", -1)
    side_b, side_a = swapped(cols_b, cols_a)

    nh, nl, ch, cl, th, tl, bands, bands_t = build(kernel_rows, kernel_cols, kernel_depth, depth)

    sides = jnp.concatenate([north, south], 0)
    corner_b, corner_a = swapped(side_cols(sides, 1 - right), side_cols(sides, right))

    partial = near((tile, north, south, side_a, side_b), nh, nl)
    to_a, to_b, bh, bl = middle(partial, corner_a, corner_b, ch, cl, bands, bands_t, th, tl, hessian)
    from_b, from_a = swapped(to_b, to_a)

    above, below, edge_a, edge_b = spread(
        1, th, tl, bh, bl, [(reach, span_cols)] * 2 + [(span_rows, reach)] * 2
    )
    edge_from_b, edge_from_a = swapped(edge_b, edge_a)

    around = jnp.concatenate([above, below], 0) + joined(from_a, from_b)
    above, below = around[:reach], around[reach:]
    side_from_n = shift(below, "gx", 1)
    above, below = lax.optimization_barrier((above, below))
    side_from_s = shift(above, "gx", -1)

    around, bh, bl = lax.optimization_barrier((around, bh, bl))
    (own,) = spread(0, th, tl, bh, bl, [(span_rows, span_cols)])
    own = lax.optimization_barrier(own + joined(edge_from_a, edge_from_b))
    return own + jnp.concatenate([side_from_n, side_from_s], 0)


def solution(mesh):
    return jax.shard_map(
        per_device,
        mesh=mesh,
        in_specs=(P("gx", "gy", None), P(None, None, "gx", "gy", None), P(), P(), P()),
        out_specs=P("gx", "gy", None),
        check_vma=False,
    )
```

```python
import functools

import jax
import jax.numpy as jnp
from jax import lax
from jax.experimental import pallas as pl
from jax.experimental.pallas import tpu as pltpu
from jax.sharding import PartitionSpec as P

RADIUS = 8
DENSITIES = 5
TAPS = 2 * RADIUS + 1
TILE = 16
CELLS = TILE * TILE


LANES = 128
TURN = TILE + RADIUS


def side_is_right():
    return 1 - lax.rem(lax.axis_index("gy"), 2)


def taps_at(weights, density, offsets):
    total = jnp.zeros(offsets.shape, jnp.float32)
    for tap in range(TAPS):
        total = jnp.where(offsets == tap - RADIUS, weights[density, tap], total)
    return total


def taps_of_all(weights, offsets):
    totals = [jnp.zeros(offsets.shape, jnp.float32)] * DENSITIES
    for tap in range(TAPS):
        here = offsets == tap - RADIUS
        totals = [jnp.where(here, weights[a, tap], totals[a]) for a in range(DENSITIES)]
    return totals


def build_kernel(
    kr_hbm, kc_hbm, kd_hbm, nh, nl, ch, cl, th, tl, bands, bands_t, kr, kc, depth_taps, depth_row, sems
):
    copies = [
        pltpu.make_async_copy(kr_hbm, kr, sems.at[0]),
        pltpu.make_async_copy(kc_hbm, kc, sems.at[1]),
        pltpu.make_async_copy(kd_hbm, depth_taps, sems.at[2]),
    ]
    for copy in copies:
        copy.start()
    copies[2].wait()
    right = side_is_right()
    iota = lambda shape, dim: lax.broadcasted_iota(jnp.int32, shape, dim)

    depth_row[...] = jnp.zeros(depth_row.shape, jnp.float32)
    depth_row[:DENSITIES, :TAPS] = depth_taps[...].astype(jnp.float32)
    depth = bands.shape[-1]
    block = (LANES, LANES)
    ahead = iota(block, 1) - iota(block, 0)

    def band(density, carry):
        row = jnp.broadcast_to(depth_row[pl.ds(density, 1)], block)
        ring_t = pltpu.roll(row, LANES - RADIUS, 1, stride=1, stride_axis=0)
        for ref, ring in ((bands_t, ring_t), (bands, ring_t.T)):
            ref[density] = jnp.zeros((depth, depth), jnp.bfloat16)
            for step in (-1, 0, 1):
                here = jnp.abs(ahead + step * LANES) <= RADIUS
                part = jnp.where(here, ring, 0.0).astype(jnp.bfloat16)
                for start in range(0, depth, LANES):
                    across = start + step * LANES
                    if 0 <= across < depth:
                        ref[density, start : start + LANES, across : across + LANES] = part
        return carry

    lax.fori_loop(0, DENSITIES, band, 0)
    for copy in copies[:2]:
        copy.wait()

    def put(high_ref, low_ref, start, lanes, values):
        high, low = halves(values)
        high_ref[start : start + TILE, lanes] = high
        low_ref[start : start + TILE, lanes] = low

    def forward(high_ref, low_ref, first):
        def chunk(index, carry):
            lanes = pl.ds(pl.multiple_of(index * LANES, LANES), LANES)
            group, half = (first + index) // 2, (first + index) % 2
            lane, tile_place = iota((TILE, LANES), 1), iota((TILE, LANES), 0)
            wide, slim = lane >> 4, lane >> 3
            row = jnp.where(group == 1, wide - RADIUS + TURN * half, slim)
            row = jnp.where(group == 0, wide + RADIUS * half, row)
            row = jnp.where(group == 3, (slim & 7) - RADIUS + TURN * half, row)
            side = jnp.where(group == 3, lane >> 6, half)
            side = side + right - 2 * side * right
            col = jnp.where(group < 2, lane & 15, (lane & 7) - RADIUS + TURN * side)
            by_row = taps_of_all(kr, row - tile_place)
            by_col = taps_of_all(kc, col - tile_place)
            for a in range(DENSITIES):
                for r in range(TILE):
                    put(high_ref, low_ref, a * CELLS + r * TILE, lanes, by_row[a][r : r + 1] * by_col[a])
            return carry

        lax.fori_loop(0, high_ref.shape[1] // LANES, chunk, 0)

    forward(nh, nl, 0)
    forward(ch, cl, 6)

    def transposes(index, carry):
        density, half = index // 2, index % 2
        lanes = pl.ds(pl.multiple_of(index * LANES, LANES), LANES)
        shape = (TILE + 2 * RADIUS, LANES)
        place, lane = iota(shape, 0), iota(shape, 1)
        turn = TURN * right
        turned = place - RADIUS + jnp.where(place < RADIUS, turn, jnp.where(place < TILE + RADIUS, 0, -turn))
        by_row = taps_at(kr, density, place - RADIUS - (lane >> 4) - RADIUS * half)
        by_col = taps_at(kc, density, turned - (lane & 15))
        row = lambda r: by_row[r + RADIUS : r + RADIUS + 1]
        inner = list(range(TILE))
        outer = list(range(-RADIUS, 0)) + list(range(TILE, TILE + RADIUS))
        mid = by_col[RADIUS : RADIUS + TILE]
        for place, r in enumerate(inner + outer):
            put(th, tl, place * TILE, lanes, row(r) * mid)
        for base, rows in ((2 * CELLS, inner), (3 * CELLS, outer)):
            for side, edge in enumerate((by_col[:RADIUS], by_col[RADIUS + TILE :])):
                for pair in range(TILE // 2):
                    both = [row(rows[2 * pair]) * edge, row(rows[2 * pair + 1]) * edge]
                    put(th, tl, base + side * CELLS // 2 + pair * TILE, lanes, jnp.concatenate(both, 0))
        return carry

    lax.fori_loop(0, DENSITIES * CELLS // LANES, transposes, 0)

def build(kernel_rows, kernel_cols, kernel_depth, depth):
    cells = DENSITIES * CELLS
    shapes = [(cells, 3 * CELLS)] * 2 + [(cells, CELLS)] * 2
    shapes += [(4 * CELLS, cells)] * 2
    shapes += [(DENSITIES, depth, depth)] * 2
    vmem = pl.BlockSpec(memory_space=pltpu.VMEM)
    hbm = pl.BlockSpec(memory_space=pltpu.HBM)
    return pl.pallas_call(
        build_kernel,
        out_shape=[jax.ShapeDtypeStruct(s, jnp.bfloat16) for s in shapes],
        in_specs=[hbm] * 3,
        out_specs=[vmem] * len(shapes),
        scratch_shapes=[
            pltpu.SMEM(kernel_rows.shape, jnp.float32),
            pltpu.SMEM(kernel_cols.shape, jnp.float32),
            pltpu.VMEM(kernel_depth.shape, jnp.bfloat16),
            pltpu.VMEM((RADIUS, LANES), jnp.float32),
            pltpu.SemaphoreType.DMA((3,)),
        ],
        compiler_params=pltpu.CompilerParams(vmem_limit_bytes=24 << 20),
        cost_estimate=pl.CostEstimate(flops=30 << 20, bytes_accessed=16 << 20, transcendentals=0),
        name="build",
    )(*[pltpu.with_memory_space_constraint(a, pltpu.HBM) for a in (kernel_rows, kernel_cols, kernel_depth)])


def halves(values):
    high = values.astype(jnp.bfloat16)
    return high, (values - high.astype(jnp.float32)).astype(jnp.bfloat16)


def dot3(left_high, left_low, right_high, right_low):
    left = jnp.concatenate([left_high, left_low, left_high], 1)
    right = jnp.concatenate([right_high, right_high, right_low], 0)
    return jnp.dot(left, right, preferred_element_type=jnp.float32)


def near_kernel(own, north, south, side_a, side_b, wh, wl, out, xh, xl):
    depth = own.shape[-1]
    start = 0
    for ref in (own, north, south, side_a, side_b):
        size = ref.shape[0] * ref.shape[1]
        high, low = halves(ref[...].reshape(size, depth))
        xh[start : start + size] = high
        xl[start : start + size] = low
        start += size

    def density(index, carry):
        rows = pl.ds(pl.multiple_of(index * CELLS, CELLS), CELLS)
        out[rows] = dot3(wh[rows], wl[rows], xh[...], xl[...])
        return carry

    lax.fori_loop(0, DENSITIES, density, 0)


def near(pieces, wh, wl):
    depth = pieces[0].shape[-1]
    keys = 3 * CELLS
    vmem = pl.BlockSpec(memory_space=pltpu.VMEM)
    return pl.pallas_call(
        near_kernel,
        out_shape=jax.ShapeDtypeStruct((DENSITIES * CELLS, depth), jnp.float32),
        in_specs=[vmem] * 7,
        out_specs=vmem,
        scratch_shapes=[pltpu.VMEM((keys, depth), jnp.bfloat16)] * 2,
        compiler_params=pltpu.CompilerParams(vmem_limit_bytes=16 << 20),
        cost_estimate=pl.CostEstimate(
            flops=6 * DENSITIES * CELLS * keys * depth, bytes_accessed=10 << 20, transcendentals=0
        ),
        name="near",
    )(*pieces, wh, wl)


def middle_kernel(
    partial, corner_a, corner_b, wh, wl, bands, bands_t, th, tl, hessian, out_a, out_b, bh, bl,
    dens, low
):
    depth = partial.shape[-1]
    half = CELLS // 2
    terms = []
    for part in range(2):
        pieces = [ref[part * RADIUS : (part + 1) * RADIUS].reshape(half // 2, depth) for ref in (corner_a, corner_b)]
        high, rest = halves(jnp.concatenate(pieces, 0))
        lanes = slice(part * half, (part + 1) * half)
        tile_rows = [slice(b * CELLS + part * half, b * CELLS + (part + 1) * half) for b in range(DENSITIES)]
        of_all = lambda ref: jnp.concatenate([ref[rows, lanes] for rows in tile_rows], 0)
        terms.append(dot3(of_all(wh), of_all(wl), high, rest))
    for b in range(DENSITIES):
        rows = slice(b * CELLS, (b + 1) * CELLS)
        own = slice(b * half, (b + 1) * half)
        lateral = partial[rows] + jnp.concatenate([terms[0][own], terms[1][own]], 0)
        dens[b] = jnp.dot(lateral.astype(jnp.bfloat16), bands[b], preferred_element_type=jnp.float32)
    for a in range(DENSITIES):
        for r in range(TILE):
            cells = slice(r * TILE, (r + 1) * TILE)
            grad = hessian[a, 0, r].astype(jnp.float32) * dens[0, cells]
            for b in range(1, DENSITIES):
                grad = grad + hessian[a, b, r].astype(jnp.float32) * dens[b, cells]
            low[a, cells] = grad.astype(jnp.bfloat16)
        back = jnp.dot(low[a], bands_t[a], preferred_element_type=jnp.float32)
        rows = slice(a * CELLS, (a + 1) * CELLS)
        high, rest = halves(back)
        bh[rows] = high
        bl[rows] = rest
    corners = slice(3 * CELLS, 4 * CELLS)
    total = dot3(th[corners], tl[corners], bh[...], bl[...])
    out_a[...] = total[:half].reshape(out_a.shape)
    out_b[...] = total[half:].reshape(out_b.shape)


def middle(partial, corner_a, corner_b, wh, wl, bands, bands_t, th, tl, hessian):
    depth = partial.shape[-1]
    edge = jax.ShapeDtypeStruct(corner_a.shape, jnp.float32)
    back = jax.ShapeDtypeStruct((DENSITIES * CELLS, depth), jnp.bfloat16)
    vmem = pl.BlockSpec(memory_space=pltpu.VMEM)
    return pl.pallas_call(
        middle_kernel,
        out_shape=[edge, edge, back, back],
        in_specs=[vmem] * 10,
        out_specs=[vmem] * 4,
        scratch_shapes=[
            pltpu.VMEM((DENSITIES, CELLS, depth), jnp.float32),
            pltpu.VMEM((DENSITIES, CELLS, depth), jnp.bfloat16),
        ],
        compiler_params=pltpu.CompilerParams(vmem_limit_bytes=24 << 20),
        cost_estimate=pl.CostEstimate(
            flops=DENSITIES * CELLS * depth * (12 * CELLS + 4 * depth), bytes_accessed=16 << 20, transcendentals=0
        ),
        name="middle",
    )(partial, corner_a, corner_b, wh, wl, bands, bands_t, th, tl, hessian)


def spread_kernel(group, th, tl, bh, bl, *outs):
    start = group * CELLS
    for first in range(0, len(outs), 2):
        pair = outs[first : first + 2]
        sizes = [out.shape[0] * out.shape[1] for out in pair]
        total = dot3(th[start : start + sum(sizes)], tl[start : start + sum(sizes)], bh[...], bl[...])
        start += sum(sizes)
        for out, size, offset in zip(pair, sizes, (0, sizes[0])):
            out[...] = total[offset : offset + size].reshape(out.shape)


def spread(group, th, tl, bh, bl, shapes):
    depth = bh.shape[-1]
    vmem = pl.BlockSpec(memory_space=pltpu.VMEM)
    return pl.pallas_call(
        functools.partial(spread_kernel, group),
        out_shape=[jax.ShapeDtypeStruct(s + (depth,), jnp.float32) for s in shapes],
        in_specs=[vmem] * 4,
        out_specs=[vmem] * len(shapes),
        compiler_params=pltpu.CompilerParams(vmem_limit_bytes=16 << 20),
        cost_estimate=pl.CostEstimate(
            flops=6 * sum(r * c for r, c in shapes) * th.shape[1] * depth, bytes_accessed=6 << 20, transcendentals=0
        ),
        name="spread",
    )(th, tl, bh, bl)


PIECES = 8


def cut_kernel(tangent, last, first, side_a, side_b, tile, sems):
    right = side_is_right()
    step = TILE // PIECES
    copies = [
        pltpu.make_async_copy(tangent.at[pl.ds(step * i, step)], tile.at[pl.ds(step * i, step)], sems.at[i])
        for i in range(PIECES)
    ]
    for copy in copies:
        copy.start()
    for copy in copies:
        copy.wait()
    cols = lambda place: pl.ds(pl.multiple_of(place * RADIUS, RADIUS), RADIUS)
    last[...] = tile[RADIUS:]
    first[...] = tile[:RADIUS]
    side_a[...] = tile[:, cols(right)]
    side_b[...] = tile[:, cols(1 - right)]


def cut(tangent):
    span_rows, span_cols, depth = tangent.shape
    shapes = [(RADIUS, span_cols)] * 2 + [(span_rows, RADIUS)] * 2 + [(span_rows, span_cols)]
    vmem = pl.BlockSpec(memory_space=pltpu.VMEM)
    return pl.pallas_call(
        cut_kernel,
        out_shape=[jax.ShapeDtypeStruct(s + (depth,), jnp.float32) for s in shapes],
        in_specs=[pl.BlockSpec(memory_space=pltpu.HBM)],
        out_specs=[vmem] * 5,
        scratch_shapes=[pltpu.SemaphoreType.DMA((PIECES,))],
        compiler_params=pltpu.CompilerParams(vmem_limit_bytes=8 << 20),
        cost_estimate=pl.CostEstimate(flops=0, bytes_accessed=3 << 20, transcendentals=0),
        name="cut",
    )(pltpu.with_memory_space_constraint(tangent, pltpu.HBM))


def shift(cells, axis, step):
    count = lax.axis_size(axis)
    return lax.ppermute(cells, axis, [(i, (i + step) % count) for i in range(count)])


def swap_a(cells):
    count = lax.axis_size("gy")
    return lax.ppermute(cells, "gy", [(j, j ^ 1) for j in range(count)])


def swap_b(cells):
    count = lax.axis_size("gy")
    return lax.ppermute(cells, "gy", [(j, (j + (1 if j % 2 else -1)) % count) for j in range(count)])


def swapped(for_b, for_a):
    from_b = swap_b(for_b)
    for_b, for_a = lax.optimization_barrier((for_b, for_a))
    return from_b, swap_a(for_a)


def per_device(tangent, hessian, kernel_rows, kernel_cols, kernel_depth):
    span_rows, span_cols, depth = tangent.shape
    reach = RADIUS
    right = side_is_right()

    def side_cols(cells, place):
        return jnp.where(place == 1, cells[:, reach:], cells[:, :reach])

    def joined(from_a, from_b):
        left, other = jnp.concatenate([from_a, from_b], 1), jnp.concatenate([from_b, from_a], 1)
        return jnp.where(right == 1, other, left)

    last, first, cols_a, cols_b, tile = cut(tangent)
    north = shift(last, "gx", 1)
    south = shift(first, "gx", -1)
    side_b, side_a = swapped(cols_b, cols_a)

    nh, nl, ch, cl, th, tl, bands, bands_t = build(kernel_rows, kernel_cols, kernel_depth, depth)

    sides = jnp.concatenate([north, south], 0)
    corner_b, corner_a = swapped(side_cols(sides, 1 - right), side_cols(sides, right))

    partial = near((tile, north, south, side_a, side_b), nh, nl)
    to_a, to_b, bh, bl = middle(partial, corner_a, corner_b, ch, cl, bands, bands_t, th, tl, hessian)
    from_b, from_a = swapped(to_b, to_a)

    above, below, edge_a, edge_b = spread(
        1, th, tl, bh, bl, [(reach, span_cols)] * 2 + [(span_rows, reach)] * 2
    )
    edge_from_b, edge_from_a = swapped(edge_b, edge_a)

    blank = jnp.zeros_like(from_a)
    around = jnp.concatenate([above, below], 0) + joined(blank, from_b)
    around = lax.optimization_barrier(around) + joined(from_a, blank)
    above, below = around[:reach], around[reach:]
    side_from_n = shift(below, "gx", 1)
    above, below = lax.optimization_barrier((above, below))
    side_from_s = shift(above, "gx", -1)

    around, bh, bl = lax.optimization_barrier((around, bh, bl))
    (own,) = spread(0, th, tl, bh, bl, [(span_rows, span_cols)])
    own = lax.optimization_barrier(own + joined(edge_from_a, edge_from_b))
    return own + jnp.concatenate([side_from_n, side_from_s], 0)


def solution(mesh):
    return jax.shard_map(
        per_device,
        mesh=mesh,
        in_specs=(P("gx", "gy", None), P(None, None, "gx", "gy", None), P(), P(), P()),
        out_specs=P("gx", "gy", None),
        check_vma=False,
    )
```

```python
import functools

import jax
import jax.numpy as jnp
from jax import lax
from jax.experimental import pallas as pl
from jax.experimental.pallas import tpu as pltpu
from jax.sharding import PartitionSpec as P

RADIUS = 8
DENSITIES = 5
TAPS = 2 * RADIUS + 1
TILE = 16
CELLS = TILE * TILE


LANES = 128
TURN = TILE + RADIUS


def side_is_right():
    return 1 - lax.rem(lax.axis_index("gy"), 2)


def taps_at(weights, density, offsets):
    total = jnp.zeros(offsets.shape, jnp.float32)
    for tap in range(TAPS):
        total = jnp.where(offsets == tap - RADIUS, weights[density, tap], total)
    return total


def taps_of_all(weights, offsets):
    totals = [jnp.zeros(offsets.shape, jnp.float32)] * DENSITIES
    for tap in range(TAPS):
        here = offsets == tap - RADIUS
        totals = [jnp.where(here, weights[a, tap], totals[a]) for a in range(DENSITIES)]
    return totals


def build_kernel(
    kr_hbm, kc_hbm, kd_hbm, nh, nl, ch, cl, th, tl, bands, bands_t, kr, kc, depth_taps, depth_row, sems
):
    copies = [
        pltpu.make_async_copy(kr_hbm, kr, sems.at[0]),
        pltpu.make_async_copy(kc_hbm, kc, sems.at[1]),
        pltpu.make_async_copy(kd_hbm, depth_taps, sems.at[2]),
    ]
    for copy in copies:
        copy.start()
    copies[2].wait()
    right = side_is_right()
    iota = lambda shape, dim: lax.broadcasted_iota(jnp.int32, shape, dim)

    depth_row[...] = jnp.zeros(depth_row.shape, jnp.float32)
    depth_row[:DENSITIES, :TAPS] = depth_taps[...].astype(jnp.float32)
    mid = bands.shape[-1]
    block = (LANES, LANES)
    ahead = iota(block, 1) - iota(block, 0)

    def band(density, carry):
        row = jnp.broadcast_to(depth_row[pl.ds(density, 1)], block)
        ring_t = pltpu.roll(row, LANES - RADIUS, 1, stride=1, stride_axis=0)
        for ref, ring in ((bands_t, ring_t), (bands, ring_t.T)):
            ref[density] = jnp.zeros(ref.shape[1:], jnp.bfloat16)
            for step in (-1, 0, 1):
                here = jnp.abs(ahead + step * LANES) <= RADIUS
                part = jnp.where(here, ring, 0.0).astype(jnp.bfloat16)
                for start in range(0, mid, LANES):
                    across = start + step * LANES
                    if 0 <= across < mid:
                        ref[density, 0, start : start + LANES, across : across + LANES] = part
                        if step:
                            ref[density, 1, start : start + LANES, across : across + LANES] = part
        return carry

    lax.fori_loop(0, DENSITIES, band, 0)
    for copy in copies[:2]:
        copy.wait()

    def put(high_ref, low_ref, start, lanes, values):
        high, low = halves(values)
        high_ref[start : start + TILE, lanes] = high
        low_ref[start : start + TILE, lanes] = low

    def forward(high_ref, low_ref, first):
        def chunk(index, carry):
            lanes = pl.ds(pl.multiple_of(index * LANES, LANES), LANES)
            group, half = (first + index) // 2, (first + index) % 2
            lane, tile_place = iota((TILE, LANES), 1), iota((TILE, LANES), 0)
            wide, slim = lane >> 4, lane >> 3
            row = jnp.where(group == 1, wide - RADIUS + TURN * half, slim)
            row = jnp.where(group == 0, wide + RADIUS * half, row)
            row = jnp.where(group == 3, (slim & 7) - RADIUS + TURN * half, row)
            side = jnp.where(group == 3, lane >> 6, half)
            side = side + right - 2 * side * right
            col = jnp.where(group < 2, lane & 15, (lane & 7) - RADIUS + TURN * side)
            by_row = taps_of_all(kr, row - tile_place)
            by_col = taps_of_all(kc, col - tile_place)
            for a in range(DENSITIES):
                for r in range(TILE):
                    put(high_ref, low_ref, a * CELLS + r * TILE, lanes, by_row[a][r : r + 1] * by_col[a])
            return carry

        lax.fori_loop(0, high_ref.shape[1] // LANES, chunk, 0)

    forward(nh, nl, 0)
    forward(ch, cl, 6)

    def transposes(index, carry):
        density, half = index // 2, index % 2
        lanes = pl.ds(pl.multiple_of(index * LANES, LANES), LANES)
        shape = (TILE + 2 * RADIUS, LANES)
        place, lane = iota(shape, 0), iota(shape, 1)
        turn = TURN * right
        turned = place - RADIUS + jnp.where(place < RADIUS, turn, jnp.where(place < TILE + RADIUS, 0, -turn))
        by_row = taps_at(kr, density, place - RADIUS - (lane >> 4) - RADIUS * half)
        by_col = taps_at(kc, density, turned - (lane & 15))
        row = lambda r: by_row[r + RADIUS : r + RADIUS + 1]
        inner = list(range(TILE))
        outer = list(range(-RADIUS, 0)) + list(range(TILE, TILE + RADIUS))
        mid = by_col[RADIUS : RADIUS + TILE]
        for place, r in enumerate(inner + outer):
            put(th, tl, place * TILE, lanes, row(r) * mid)
        for base, rows in ((2 * CELLS, inner), (3 * CELLS, outer)):
            for side, edge in enumerate((by_col[:RADIUS], by_col[RADIUS + TILE :])):
                for pair in range(TILE // 2):
                    both = [row(rows[2 * pair]) * edge, row(rows[2 * pair + 1]) * edge]
                    put(th, tl, base + side * CELLS // 2 + pair * TILE, lanes, jnp.concatenate(both, 0))
        return carry

    lax.fori_loop(0, DENSITIES * CELLS // LANES, transposes, 0)

def build(kernel_rows, kernel_cols, kernel_depth, depth):
    cells = DENSITIES * CELLS
    shapes = [(cells, 3 * CELLS)] * 2 + [(cells, CELLS)] * 2
    shapes += [(4 * CELLS, cells)] * 2
    shapes += [(DENSITIES, 2, depth // 2, depth // 2)] * 2
    vmem = pl.BlockSpec(memory_space=pltpu.VMEM)
    hbm = pl.BlockSpec(memory_space=pltpu.HBM)
    return pl.pallas_call(
        build_kernel,
        out_shape=[jax.ShapeDtypeStruct(s, jnp.bfloat16) for s in shapes],
        in_specs=[hbm] * 3,
        out_specs=[vmem] * len(shapes),
        scratch_shapes=[
            pltpu.SMEM(kernel_rows.shape, jnp.float32),
            pltpu.SMEM(kernel_cols.shape, jnp.float32),
            pltpu.VMEM(kernel_depth.shape, jnp.bfloat16),
            pltpu.VMEM((RADIUS, LANES), jnp.float32),
            pltpu.SemaphoreType.DMA((3,)),
        ],
        compiler_params=pltpu.CompilerParams(vmem_limit_bytes=24 << 20),
        cost_estimate=pl.CostEstimate(flops=30 << 20, bytes_accessed=16 << 20, transcendentals=0),
        name="build",
    )(*[pltpu.with_memory_space_constraint(a, pltpu.HBM) for a in (kernel_rows, kernel_cols, kernel_depth)])


def halves(values):
    high = values.astype(jnp.bfloat16)
    return high, (values - high.astype(jnp.float32)).astype(jnp.bfloat16)


def dot3(left_high, left_low, right_high, right_low):
    left = jnp.concatenate([left_high, left_low, left_high], 1)
    right = jnp.concatenate([right_high, right_high, right_low], 0)
    return jnp.dot(left, right, preferred_element_type=jnp.float32)


def near_kernel(own, north, south, side_a, side_b, wh, wl, out, xh, xl):
    depth = own.shape[-1]
    start = 0
    for ref in (own, north, south, side_a, side_b):
        size = ref.shape[0] * ref.shape[1]
        high, low = halves(ref[...].reshape(size, depth))
        xh[start : start + size] = high
        xl[start : start + size] = low
        start += size

    def density(index, carry):
        rows = pl.ds(pl.multiple_of(index * CELLS, CELLS), CELLS)
        out[rows] = dot3(wh[rows], wl[rows], xh[...], xl[...])
        return carry

    lax.fori_loop(0, DENSITIES, density, 0)


def near(pieces, wh, wl):
    depth = pieces[0].shape[-1]
    keys = 3 * CELLS
    vmem = pl.BlockSpec(memory_space=pltpu.VMEM)
    return pl.pallas_call(
        near_kernel,
        out_shape=jax.ShapeDtypeStruct((DENSITIES * CELLS, depth), jnp.float32),
        in_specs=[vmem] * 7,
        out_specs=vmem,
        scratch_shapes=[pltpu.VMEM((keys, depth), jnp.bfloat16)] * 2,
        compiler_params=pltpu.CompilerParams(vmem_limit_bytes=16 << 20),
        cost_estimate=pl.CostEstimate(
            flops=6 * DENSITIES * CELLS * keys * depth, bytes_accessed=10 << 20, transcendentals=0
        ),
        name="near",
    )(*pieces, wh, wl)


def along_depth(values, bands):
    mid, count = bands.shape[-1], values.shape[0]
    quarter = mid // 2
    stacked = jnp.concatenate([values[:, :mid], values[:, mid:]], 0)
    main = jnp.dot(stacked, bands[0], preferred_element_type=jnp.float32)
    cross = jnp.dot(values[:, quarter : quarter + mid], bands[1], preferred_element_type=jnp.float32)
    first, second = main[:count], main[count:]
    parts = [
        first[:, :quarter],
        first[:, quarter:] + cross[:, :quarter],
        second[:, :quarter] + cross[:, quarter:],
        second[:, quarter:],
    ]
    return jnp.concatenate(parts, 1)


def middle_kernel(
    partial, corner_a, corner_b, wh, wl, bands, bands_t, th, tl, hessian, out_a, out_b, bh, bl,
    dens, low
):
    depth = partial.shape[-1]
    half = CELLS // 2
    terms = []
    for part in range(2):
        pieces = [ref[part * RADIUS : (part + 1) * RADIUS].reshape(half // 2, depth) for ref in (corner_a, corner_b)]
        high, rest = halves(jnp.concatenate(pieces, 0))
        lanes = slice(part * half, (part + 1) * half)
        tile_rows = [slice(b * CELLS + part * half, b * CELLS + (part + 1) * half) for b in range(DENSITIES)]
        of_all = lambda ref: jnp.concatenate([ref[rows, lanes] for rows in tile_rows], 0)
        terms.append(dot3(of_all(wh), of_all(wl), high, rest))
    for b in range(DENSITIES):
        rows = slice(b * CELLS, (b + 1) * CELLS)
        own = slice(b * half, (b + 1) * half)
        lateral = partial[rows] + jnp.concatenate([terms[0][own], terms[1][own]], 0)
        dens[b] = along_depth(lateral.astype(jnp.bfloat16), bands[b])
    for a in range(DENSITIES):
        for r in range(TILE):
            cells = slice(r * TILE, (r + 1) * TILE)
            grad = hessian[a, 0, r].astype(jnp.float32) * dens[0, cells]
            for b in range(1, DENSITIES):
                grad = grad + hessian[a, b, r].astype(jnp.float32) * dens[b, cells]
            low[a, cells] = grad.astype(jnp.bfloat16)
        back = along_depth(low[a], bands_t[a])
        rows = slice(a * CELLS, (a + 1) * CELLS)
        high, rest = halves(back)
        bh[rows] = high
        bl[rows] = rest
    corners = slice(3 * CELLS, 4 * CELLS)
    total = dot3(th[corners], tl[corners], bh[...], bl[...])
    out_a[...] = total[:half].reshape(out_a.shape)
    out_b[...] = total[half:].reshape(out_b.shape)


def middle(partial, corner_a, corner_b, wh, wl, bands, bands_t, th, tl, hessian):
    depth = partial.shape[-1]
    edge = jax.ShapeDtypeStruct(corner_a.shape, jnp.float32)
    back = jax.ShapeDtypeStruct((DENSITIES * CELLS, depth), jnp.bfloat16)
    vmem = pl.BlockSpec(memory_space=pltpu.VMEM)
    return pl.pallas_call(
        middle_kernel,
        out_shape=[edge, edge, back, back],
        in_specs=[vmem] * 10,
        out_specs=[vmem] * 4,
        scratch_shapes=[
            pltpu.VMEM((DENSITIES, CELLS, depth), jnp.float32),
            pltpu.VMEM((DENSITIES, CELLS, depth), jnp.bfloat16),
        ],
        compiler_params=pltpu.CompilerParams(vmem_limit_bytes=24 << 20),
        cost_estimate=pl.CostEstimate(
            flops=DENSITIES * CELLS * depth * (12 * CELLS + 4 * depth), bytes_accessed=16 << 20, transcendentals=0
        ),
        name="middle",
    )(partial, corner_a, corner_b, wh, wl, bands, bands_t, th, tl, hessian)


def spread_kernel(group, th, tl, bh, bl, *outs):
    start = group * CELLS
    for first in range(0, len(outs), 2):
        pair = outs[first : first + 2]
        sizes = [out.shape[0] * out.shape[1] for out in pair]
        total = dot3(th[start : start + sum(sizes)], tl[start : start + sum(sizes)], bh[...], bl[...])
        start += sum(sizes)
        for out, size, offset in zip(pair, sizes, (0, sizes[0])):
            out[...] = total[offset : offset + size].reshape(out.shape)


def spread(group, th, tl, bh, bl, shapes):
    depth = bh.shape[-1]
    vmem = pl.BlockSpec(memory_space=pltpu.VMEM)
    return pl.pallas_call(
        functools.partial(spread_kernel, group),
        out_shape=[jax.ShapeDtypeStruct(s + (depth,), jnp.float32) for s in shapes],
        in_specs=[vmem] * 4,
        out_specs=[vmem] * len(shapes),
        compiler_params=pltpu.CompilerParams(vmem_limit_bytes=16 << 20),
        cost_estimate=pl.CostEstimate(
            flops=6 * sum(r * c for r, c in shapes) * th.shape[1] * depth, bytes_accessed=6 << 20, transcendentals=0
        ),
        name="spread",
    )(th, tl, bh, bl)


PIECES = 8


def cut_kernel(tangent, last, first, side_a, side_b, tile, sems):
    right = side_is_right()
    step = TILE // PIECES
    copies = [
        pltpu.make_async_copy(tangent.at[pl.ds(step * i, step)], tile.at[pl.ds(step * i, step)], sems.at[i])
        for i in range(PIECES)
    ]
    for copy in copies:
        copy.start()
    for copy in copies:
        copy.wait()
    cols = lambda place: pl.ds(pl.multiple_of(place * RADIUS, RADIUS), RADIUS)
    last[...] = tile[RADIUS:]
    first[...] = tile[:RADIUS]
    side_a[...] = tile[:, cols(right)]
    side_b[...] = tile[:, cols(1 - right)]


def cut(tangent):
    span_rows, span_cols, depth = tangent.shape
    shapes = [(RADIUS, span_cols)] * 2 + [(span_rows, RADIUS)] * 2 + [(span_rows, span_cols)]
    vmem = pl.BlockSpec(memory_space=pltpu.VMEM)
    return pl.pallas_call(
        cut_kernel,
        out_shape=[jax.ShapeDtypeStruct(s + (depth,), jnp.float32) for s in shapes],
        in_specs=[pl.BlockSpec(memory_space=pltpu.HBM)],
        out_specs=[vmem] * 5,
        scratch_shapes=[pltpu.SemaphoreType.DMA((PIECES,))],
        compiler_params=pltpu.CompilerParams(vmem_limit_bytes=8 << 20),
        cost_estimate=pl.CostEstimate(flops=0, bytes_accessed=3 << 20, transcendentals=0),
        name="cut",
    )(pltpu.with_memory_space_constraint(tangent, pltpu.HBM))


def shift(cells, axis, step):
    count = lax.axis_size(axis)
    return lax.ppermute(cells, axis, [(i, (i + step) % count) for i in range(count)])


def swap_a(cells):
    count = lax.axis_size("gy")
    return lax.ppermute(cells, "gy", [(j, j ^ 1) for j in range(count)])


def swap_b(cells):
    count = lax.axis_size("gy")
    return lax.ppermute(cells, "gy", [(j, (j + (1 if j % 2 else -1)) % count) for j in range(count)])


def swapped(for_b, for_a):
    from_b = swap_b(for_b)
    for_b, for_a = lax.optimization_barrier((for_b, for_a))
    return from_b, swap_a(for_a)


def per_device(tangent, hessian, kernel_rows, kernel_cols, kernel_depth):
    span_rows, span_cols, depth = tangent.shape
    reach = RADIUS
    right = side_is_right()

    def side_cols(cells, place):
        return jnp.where(place == 1, cells[:, reach:], cells[:, :reach])

    def joined(from_a, from_b):
        left, other = jnp.concatenate([from_a, from_b], 1), jnp.concatenate([from_b, from_a], 1)
        return jnp.where(right == 1, other, left)

    last, first, cols_a, cols_b, tile = cut(tangent)
    north = shift(last, "gx", 1)
    south = shift(first, "gx", -1)
    side_b, side_a = swapped(cols_b, cols_a)

    nh, nl, ch, cl, th, tl, bands, bands_t = build(kernel_rows, kernel_cols, kernel_depth, depth)

    sides = jnp.concatenate([north, south], 0)
    corner_b, corner_a = swapped(side_cols(sides, 1 - right), side_cols(sides, right))

    partial = near((tile, north, south, side_a, side_b), nh, nl)
    to_a, to_b, bh, bl = middle(partial, corner_a, corner_b, ch, cl, bands, bands_t, th, tl, hessian)
    from_b, from_a = swapped(to_b, to_a)

    above, below, edge_a, edge_b = spread(
        1, th, tl, bh, bl, [(reach, span_cols)] * 2 + [(span_rows, reach)] * 2
    )
    edge_from_b, edge_from_a = swapped(edge_b, edge_a)

    blank = jnp.zeros_like(from_a)
    around = jnp.concatenate([above, below], 0) + joined(blank, from_b)
    around = lax.optimization_barrier(around) + joined(from_a, blank)
    above, below = around[:reach], around[reach:]
    side_from_n = shift(below, "gx", 1)
    above, below = lax.optimization_barrier((above, below))
    side_from_s = shift(above, "gx", -1)

    around, bh, bl = lax.optimization_barrier((around, bh, bl))
    (own,) = spread(0, th, tl, bh, bl, [(span_rows, span_cols)])
    own = lax.optimization_barrier(own + joined(edge_from_a, edge_from_b))
    return own + jnp.concatenate([side_from_n, side_from_s], 0)


def solution(mesh):
    return jax.shard_map(
        per_device,
        mesh=mesh,
        in_specs=(P("gx", "gy", None), P(None, None, "gx", "gy", None), P(), P(), P()),
        out_specs=P("gx", "gy", None),
        check_vma=False,
    )
```

```python
import functools

import jax
import jax.numpy as jnp
from jax import lax
from jax.experimental import pallas as pl
from jax.experimental.pallas import tpu as pltpu
from jax.sharding import PartitionSpec as P

RADIUS = 8
DENSITIES = 5
TAPS = 2 * RADIUS + 1
TILE = 16
CELLS = TILE * TILE


LANES = 128
TURN = TILE + RADIUS


def side_is_right():
    return 1 - lax.rem(lax.axis_index("gy"), 2)


def taps_at(weights, density, offsets):
    total = jnp.zeros(offsets.shape, jnp.float32)
    for tap in range(TAPS):
        total = jnp.where(offsets == tap - RADIUS, weights[density, tap], total)
    return total


def taps_of_all(weights, offsets):
    totals = [jnp.zeros(offsets.shape, jnp.float32)] * DENSITIES
    for tap in range(TAPS):
        here = offsets == tap - RADIUS
        totals = [jnp.where(here, weights[a, tap], totals[a]) for a in range(DENSITIES)]
    return totals


def build_kernel(
    kr_hbm, kc_hbm, kd_hbm, nh, nl, ch, cl, th, tl, bands, bands_t, kr, kc, depth_taps, depth_row, sems
):
    copies = [
        pltpu.make_async_copy(kr_hbm, kr, sems.at[0]),
        pltpu.make_async_copy(kc_hbm, kc, sems.at[1]),
        pltpu.make_async_copy(kd_hbm, depth_taps, sems.at[2]),
    ]
    for copy in copies:
        copy.start()
    copies[2].wait()
    right = side_is_right()
    iota = lambda shape, dim: lax.broadcasted_iota(jnp.int32, shape, dim)

    depth_row[...] = jnp.zeros(depth_row.shape, jnp.float32)
    depth_row[:DENSITIES, :TAPS] = depth_taps[...].astype(jnp.float32)
    mid = bands.shape[-1]
    block = (LANES, LANES)
    ahead = iota(block, 1) - iota(block, 0)

    def band(density, carry):
        row = jnp.broadcast_to(depth_row[pl.ds(density, 1)], block)
        ring_t = pltpu.roll(row, LANES - RADIUS, 1, stride=1, stride_axis=0)
        for ref, ring in ((bands_t, ring_t), (bands, ring_t.T)):
            ref[density] = jnp.zeros(ref.shape[1:], jnp.bfloat16)
            for step in (-1, 0, 1):
                here = jnp.abs(ahead + step * LANES) <= RADIUS
                part = jnp.where(here, ring, 0.0).astype(jnp.bfloat16)
                for start in range(0, mid, LANES):
                    across = start + step * LANES
                    if 0 <= across < mid:
                        ref[density, 0, start : start + LANES, across : across + LANES] = part
                        if step:
                            ref[density, 1, start : start + LANES, across : across + LANES] = part
        return carry

    lax.fori_loop(0, DENSITIES, band, 0)
    for copy in copies[:2]:
        copy.wait()

    def put(high_ref, low_ref, start, lanes, values):
        high, low = halves(values)
        high_ref[start : start + TILE, lanes] = high
        low_ref[start : start + TILE, lanes] = low

    def forward(high_ref, low_ref, first):
        def chunk(index, carry):
            lanes = pl.ds(pl.multiple_of(index * LANES, LANES), LANES)
            group, half = (first + index) // 2, (first + index) % 2
            lane, tile_place = iota((TILE, LANES), 1), iota((TILE, LANES), 0)
            wide, slim = lane >> 4, lane >> 3
            row = jnp.where(group == 1, wide - RADIUS + TURN * half, slim)
            row = jnp.where(group == 0, wide + RADIUS * half, row)
            row = jnp.where(group == 3, (slim & 7) - RADIUS + TURN * half, row)
            side = jnp.where(group == 3, lane >> 6, half)
            side = side + right - 2 * side * right
            col = jnp.where(group < 2, lane & 15, (lane & 7) - RADIUS + TURN * side)
            by_row = taps_of_all(kr, row - tile_place)
            by_col = taps_of_all(kc, col - tile_place)
            for a in range(DENSITIES):
                for r in range(TILE):
                    put(high_ref, low_ref, a * CELLS + r * TILE, lanes, by_row[a][r : r + 1] * by_col[a])
            return carry

        lax.fori_loop(0, high_ref.shape[1] // LANES, chunk, 0)

    forward(nh, nl, 0)
    forward(ch, cl, 6)

    def transposes(index, carry):
        density, half = index // 2, index % 2
        lanes = pl.ds(pl.multiple_of(index * LANES, LANES), LANES)
        shape = (TILE + 2 * RADIUS, LANES)
        place, lane = iota(shape, 0), iota(shape, 1)
        turn = TURN * right
        turned = place - RADIUS + jnp.where(place < RADIUS, turn, jnp.where(place < TILE + RADIUS, 0, -turn))
        by_row = taps_at(kr, density, place - RADIUS - (lane >> 4) - RADIUS * half)
        by_col = taps_at(kc, density, turned - (lane & 15))
        row = lambda r: by_row[r + RADIUS : r + RADIUS + 1]
        inner = list(range(TILE))
        outer = list(range(-RADIUS, 0)) + list(range(TILE, TILE + RADIUS))
        mid = by_col[RADIUS : RADIUS + TILE]
        for place, r in enumerate(inner + outer):
            put(th, tl, place * TILE, lanes, row(r) * mid)
        for base, rows in ((2 * CELLS, inner), (3 * CELLS, outer)):
            for side, edge in enumerate((by_col[:RADIUS], by_col[RADIUS + TILE :])):
                for pair in range(TILE // 2):
                    both = [row(rows[2 * pair]) * edge, row(rows[2 * pair + 1]) * edge]
                    put(th, tl, base + side * CELLS // 2 + pair * TILE, lanes, jnp.concatenate(both, 0))
        return carry

    lax.fori_loop(0, DENSITIES * CELLS // LANES, transposes, 0)

def build(kernel_rows, kernel_cols, kernel_depth, depth):
    cells = DENSITIES * CELLS
    shapes = [(cells, 3 * CELLS)] * 2 + [(cells, CELLS)] * 2
    shapes += [(4 * CELLS, cells)] * 2
    shapes += [(DENSITIES, 2, depth // 2, depth // 2)] * 2
    vmem = pl.BlockSpec(memory_space=pltpu.VMEM)
    hbm = pl.BlockSpec(memory_space=pltpu.HBM)
    return pl.pallas_call(
        build_kernel,
        out_shape=[jax.ShapeDtypeStruct(s, jnp.bfloat16) for s in shapes],
        in_specs=[hbm] * 3,
        out_specs=[vmem] * len(shapes),
        scratch_shapes=[
            pltpu.SMEM(kernel_rows.shape, jnp.float32),
            pltpu.SMEM(kernel_cols.shape, jnp.float32),
            pltpu.VMEM(kernel_depth.shape, jnp.bfloat16),
            pltpu.VMEM((RADIUS, LANES), jnp.float32),
            pltpu.SemaphoreType.DMA((3,)),
        ],
        compiler_params=pltpu.CompilerParams(vmem_limit_bytes=24 << 20),
        cost_estimate=pl.CostEstimate(flops=30 << 20, bytes_accessed=16 << 20, transcendentals=0),
        name="build",
    )(*[pltpu.with_memory_space_constraint(a, pltpu.HBM) for a in (kernel_rows, kernel_cols, kernel_depth)])


def halves(values):
    high = values.astype(jnp.bfloat16)
    return high, (values - high.astype(jnp.float32)).astype(jnp.bfloat16)


def dot3(left_high, left_low, right_high, right_low):
    left = jnp.concatenate([left_high, left_low, left_high], 1)
    right = jnp.concatenate([right_high, right_high, right_low], 0)
    return jnp.dot(left, right, preferred_element_type=jnp.float32)


def near_kernel(own, north, south, side_a, side_b, wh, wl, out, xh, xl):
    depth = own.shape[-1]
    start = 0
    for ref in (own, north, south, side_a, side_b):
        size = ref.shape[0] * ref.shape[1]
        high, low = halves(ref[...].reshape(size, depth))
        xh[start : start + size] = high
        xl[start : start + size] = low
        start += size

    def density(index, carry):
        rows = pl.ds(pl.multiple_of(index * CELLS, CELLS), CELLS)
        out[rows] = dot3(wh[rows], wl[rows], xh[...], xl[...])
        return carry

    lax.fori_loop(0, DENSITIES, density, 0)


def near(pieces, wh, wl):
    depth = pieces[0].shape[-1]
    keys = 3 * CELLS
    vmem = pl.BlockSpec(memory_space=pltpu.VMEM)
    return pl.pallas_call(
        near_kernel,
        out_shape=jax.ShapeDtypeStruct((DENSITIES * CELLS, depth), jnp.float32),
        in_specs=[vmem] * 7,
        out_specs=vmem,
        scratch_shapes=[pltpu.VMEM((keys, depth), jnp.bfloat16)] * 2,
        compiler_params=pltpu.CompilerParams(vmem_limit_bytes=16 << 20),
        cost_estimate=pl.CostEstimate(
            flops=6 * DENSITIES * CELLS * keys * depth, bytes_accessed=10 << 20, transcendentals=0
        ),
        name="near",
    )(*pieces, wh, wl)


def along_depth(values, bands):
    mid, count = bands.shape[-1], values.shape[0]
    quarter = mid // 2
    stacked = jnp.concatenate([values[:, :mid], values[:, mid:]], 0)
    main = jnp.dot(stacked, bands[0], preferred_element_type=jnp.float32)
    cross = jnp.dot(values[:, quarter : quarter + mid], bands[1], preferred_element_type=jnp.float32)
    first, second = main[:count], main[count:]
    parts = [
        first[:, :quarter],
        first[:, quarter:] + cross[:, :quarter],
        second[:, :quarter] + cross[:, quarter:],
        second[:, quarter:],
    ]
    return jnp.concatenate(parts, 1)


def middle_kernel(
    partial, corner_a, corner_b, wh, wl, bands, bands_t, th, tl, hessian, out_a, out_b, bh, bl,
    dens, low
):
    depth = partial.shape[-1]
    half = CELLS // 2
    terms = []
    for part in range(2):
        pieces = [ref[part * RADIUS : (part + 1) * RADIUS].reshape(half // 2, depth) for ref in (corner_a, corner_b)]
        high, rest = halves(jnp.concatenate(pieces, 0))
        lanes = slice(part * half, (part + 1) * half)
        tile_rows = [slice(b * CELLS + part * half, b * CELLS + (part + 1) * half) for b in range(DENSITIES)]
        of_all = lambda ref: jnp.concatenate([ref[rows, lanes] for rows in tile_rows], 0)
        terms.append(dot3(of_all(wh), of_all(wl), high, rest))
    for b in range(DENSITIES):
        rows = slice(b * CELLS, (b + 1) * CELLS)
        own = slice(b * half, (b + 1) * half)
        lateral = partial[rows] + jnp.concatenate([terms[0][own], terms[1][own]], 0)
        dens[b] = along_depth(lateral.astype(jnp.bfloat16), bands[b])
    for a in range(DENSITIES):
        for r in range(TILE):
            cells = slice(r * TILE, (r + 1) * TILE)
            grad = hessian[a, 0, r].astype(jnp.float32) * dens[0, cells]
            for b in range(1, DENSITIES):
                grad = grad + hessian[a, b, r].astype(jnp.float32) * dens[b, cells]
            low[a, cells] = grad.astype(jnp.bfloat16)
        back = along_depth(low[a], bands_t[a])
        rows = slice(a * CELLS, (a + 1) * CELLS)
        high, rest = halves(back)
        bh[rows] = high
        bl[rows] = rest
    corners = slice(3 * CELLS, 4 * CELLS)
    total = dot3(th[corners], tl[corners], bh[...], bl[...])
    out_a[...] = total[:half].reshape(out_a.shape)
    out_b[...] = total[half:].reshape(out_b.shape)


def middle(partial, corner_a, corner_b, wh, wl, bands, bands_t, th, tl, hessian):
    depth = partial.shape[-1]
    edge = jax.ShapeDtypeStruct(corner_a.shape, jnp.float32)
    back = jax.ShapeDtypeStruct((DENSITIES * CELLS, depth), jnp.bfloat16)
    vmem = pl.BlockSpec(memory_space=pltpu.VMEM)
    return pl.pallas_call(
        middle_kernel,
        out_shape=[edge, edge, back, back],
        in_specs=[vmem] * 10,
        out_specs=[vmem] * 4,
        scratch_shapes=[
            pltpu.VMEM((DENSITIES, CELLS, depth), jnp.float32),
            pltpu.VMEM((DENSITIES, CELLS, depth), jnp.bfloat16),
        ],
        compiler_params=pltpu.CompilerParams(vmem_limit_bytes=24 << 20),
        cost_estimate=pl.CostEstimate(
            flops=DENSITIES * CELLS * depth * (12 * CELLS + 4 * depth), bytes_accessed=16 << 20, transcendentals=0
        ),
        name="middle",
    )(partial, corner_a, corner_b, wh, wl, bands, bands_t, th, tl, hessian)


def spread_kernel(group, th, tl, bh, bl, *outs):
    start = group * CELLS
    for first in range(0, len(outs), 2):
        pair = outs[first : first + 2]
        sizes = [out.shape[0] * out.shape[1] for out in pair]
        total = dot3(th[start : start + sum(sizes)], tl[start : start + sum(sizes)], bh[...], bl[...])
        start += sum(sizes)
        for out, size, offset in zip(pair, sizes, (0, sizes[0])):
            out[...] = total[offset : offset + size].reshape(out.shape)


def spread(group, th, tl, bh, bl, shapes):
    depth = bh.shape[-1]
    vmem = pl.BlockSpec(memory_space=pltpu.VMEM)
    return pl.pallas_call(
        functools.partial(spread_kernel, group),
        out_shape=[jax.ShapeDtypeStruct(s + (depth,), jnp.float32) for s in shapes],
        in_specs=[vmem] * 4,
        out_specs=[vmem] * len(shapes),
        compiler_params=pltpu.CompilerParams(vmem_limit_bytes=16 << 20),
        cost_estimate=pl.CostEstimate(
            flops=6 * sum(r * c for r, c in shapes) * th.shape[1] * depth, bytes_accessed=6 << 20, transcendentals=0
        ),
        name="spread",
    )(th, tl, bh, bl)


PIECES = 8


def cut_kernel(tangent, last, first, side_a, side_b, tile, sems):
    right = side_is_right()
    step = TILE // PIECES
    copies = [
        pltpu.make_async_copy(tangent.at[pl.ds(step * i, step)], tile.at[pl.ds(step * i, step)], sems.at[i])
        for i in range(PIECES)
    ]
    for copy in copies:
        copy.start()
    for copy in copies:
        copy.wait()
    cols = lambda place: pl.ds(pl.multiple_of(place * RADIUS, RADIUS), RADIUS)
    last[...] = tile[RADIUS:]
    first[...] = tile[:RADIUS]
    side_a[...] = tile[:, cols(right)]
    side_b[...] = tile[:, cols(1 - right)]


def cut(tangent):
    span_rows, span_cols, depth = tangent.shape
    shapes = [(RADIUS, span_cols)] * 2 + [(span_rows, RADIUS)] * 2 + [(span_rows, span_cols)]
    vmem = pl.BlockSpec(memory_space=pltpu.VMEM)
    return pl.pallas_call(
        cut_kernel,
        out_shape=[jax.ShapeDtypeStruct(s + (depth,), jnp.float32) for s in shapes],
        in_specs=[pl.BlockSpec(memory_space=pltpu.HBM)],
        out_specs=[vmem] * 5,
        scratch_shapes=[pltpu.SemaphoreType.DMA((PIECES,))],
        compiler_params=pltpu.CompilerParams(vmem_limit_bytes=8 << 20),
        cost_estimate=pl.CostEstimate(flops=0, bytes_accessed=3 << 20, transcendentals=0),
        name="cut",
    )(pltpu.with_memory_space_constraint(tangent, pltpu.HBM))


def shift(cells, axis, step):
    count = lax.axis_size(axis)
    return lax.ppermute(cells, axis, [(i, (i + step) % count) for i in range(count)])


def swap_a(cells):
    count = lax.axis_size("gy")
    return lax.ppermute(cells, "gy", [(j, j ^ 1) for j in range(count)])


def swap_b(cells):
    count = lax.axis_size("gy")
    return lax.ppermute(cells, "gy", [(j, (j + (1 if j % 2 else -1)) % count) for j in range(count)])


def swapped(for_b, for_a):
    from_b = swap_b(for_b)
    for_b, for_a = lax.optimization_barrier((for_b, for_a))
    return from_b, swap_a(for_a)


def per_device(tangent, hessian, kernel_rows, kernel_cols, kernel_depth):
    span_rows, span_cols, depth = tangent.shape
    reach = RADIUS
    right = side_is_right()

    def side_cols(cells, place):
        return jnp.where(place == 1, cells[:, reach:], cells[:, :reach])

    def joined(from_a, from_b):
        left, other = jnp.concatenate([from_a, from_b], 1), jnp.concatenate([from_b, from_a], 1)
        return jnp.where(right == 1, other, left)

    last, first, cols_a, cols_b, tile = cut(tangent)
    north = shift(last, "gx", 1)
    south = shift(first, "gx", -1)
    side_b, side_a = swapped(cols_b, cols_a)

    nh, nl, ch, cl, th, tl, bands, bands_t = build(kernel_rows, kernel_cols, kernel_depth, depth)

    sides = jnp.concatenate([north, south], 0)
    corner_b, corner_a = swapped(side_cols(sides, 1 - right), side_cols(sides, right))

    partial = near((tile, north, south, side_a, side_b), nh, nl)
    to_a, to_b, bh, bl = middle(partial, corner_a, corner_b, ch, cl, bands, bands_t, th, tl, hessian)
    from_b, from_a = swapped(to_b, to_a)

    upper, lower, above, below, edge_a, edge_b = spread(
        0, th, tl, bh, bl, [(reach, span_cols)] * 4 + [(span_rows, reach)] * 2
    )
    edge_from_b, edge_from_a = swapped(edge_b, edge_a)

    blank = jnp.zeros_like(from_a)
    around = jnp.concatenate([above, below], 0) + joined(blank, from_b)
    around = lax.optimization_barrier(around) + joined(from_a, blank)
    above, below = around[:reach], around[reach:]
    side_from_n = shift(below, "gx", 1)
    above, below = lax.optimization_barrier((above, below))
    side_from_s = shift(above, "gx", -1)

    own = jnp.concatenate([upper, lower], 0)
    own = lax.optimization_barrier(own + joined(edge_from_a, edge_from_b))
    blank = jnp.zeros_like(side_from_n)
    own = lax.optimization_barrier(own + jnp.concatenate([side_from_n, blank], 0))
    return own + jnp.concatenate([blank, side_from_s], 0)


def solution(mesh):
    return jax.shard_map(
        per_device,
        mesh=mesh,
        in_specs=(P("gx", "gy", None), P(None, None, "gx", "gy", None), P(), P(), P()),
        out_specs=P("gx", "gy", None),
        check_vma=False,
    )
```
